128 devices in a mesh: grp: 2 (over core), blk: 64 (over x, y, z).
Axes of the slice: x: 4, y: 4, z: 4, core: 2. Of those that a mesh axis runs over, the one named last changes fastest.
Arguments:
- columns: float32 [2, 64, 1048576], P('grp', None, 'blk'), may hold values from -6 to 6
- operators: float32 [2, 64, 64], P('grp'), may hold values from -1 to 1, as said below
- normal_weights: float32 [2, 64], replicated, may hold values from -0.75 to 0.75
- face_patch: int32 [1048576, 1], P('blk'), may hold values from 0 to 63; in each aligned block of 16384 rows (0 to 16383, 16384 to 32767, ...) at most 512 rows name the same one
- face_point: int32 [1048576], P('blk'), may hold values from 0 to 16383
- live_count: int32 [64], P('blk'), may hold values from 1 to 16384, 917504 in all
- impinged: int32 [1048576], P('blk'), may hold values 0 or 1
- crystal_load: float32 [1048576], P('blk'), may hold values from 0.2 to 2
- film: float32 [1048576], P('blk'), may hold values from 0.05 to 1
Outputs:
- new_columns: float32 [2, 64, 1048576], P('grp', None, 'blk')
- surface: float32 [2, 2, 1048576], P('grp', None, 'blk')
The draws below stay inside these ranges and needn't reach their ends.
Inputs may be any that keep to these rules, and one draw needn't show every extreme that they name: `face_patch`: among the faces of one gas block (aligned blocks of 16384 rows) no patch is named more than 512 times. `operators`: diagonal entries lie in 0.5 to 1.
All inputs are finite; a program needn't handle non-finite values. No bound on the sum of `live_count` or of `impinged` on one device may be relied on, other than what follows from the above.
Results may differ from the reference program's by a relative error of at most 0.0001.
Values sent between devices are 32-bit elements; how exact they have to be, the bound alone decides.
No kernel may reach another device: no remote copies, remote signals or barrier semaphores. Data moves between devices by JAX's collectives and lax.ppermute only.
A program may use at most 128 MiB of HBM per device.

```python
import math
import jax
import jax.numpy as jnp
import numpy as np
from jax import lax

NL = 64
S = 16384
ITERS = 4
CAP = 512
FACES = 1048576
N_GRP = 2
N_BLK = 64


def draw_operators(key, part):
    first, second = jax.random.split(key)
    diagonal = jax.random.uniform(first, (N_GRP, NL), jnp.float32, 0.5, 1.0)
    spread = 0.25 * jax.random.normal(second, (N_GRP, NL, NL), jnp.float32) / math.sqrt(NL)
    identity = jnp.eye(NL, dtype=jnp.float32)
    return spread * (1.0 - identity) + diagonal[:, :, None] * identity


def plant(result, stream_key, smallest, top_value):
    longest = result.shape.index(max(result.shape))
    spots = []
    for shift in (0, 1):
        where = [jax.random.randint(jax.random.fold_in(stream_key, axis), (), 0, length) for axis, length in enumerate(result.shape)]
        where[longest] = (where[longest] + shift) % result.shape[longest]
        spots.append(tuple(where))
    return result.at[spots[0]].set(smallest).at[spots[1]].set(top_value)


def shard_levels(stream_key, shape, cuts, least, largest):
    def one(dim, shards_of):
        steps = jax.random.uniform(jax.random.fold_in(jax.random.fold_in(stream_key, 6), dim), (shards_of,), jnp.float32, least / len(cuts), largest / len(cuts))
        return jnp.repeat(jnp.exp(steps), shape[dim] // shards_of).reshape((-1,) + (1,) * (len(shape) - dim - 1))

    loudness = one(*cuts[0])
    for cut in cuts[1:]:
        loudness = loudness * one(*cut)
    return loudness


def profile(number_of, total, bound, skew):
    portions = [(1 << 20) // math.isqrt(standing ** skew) + 1 for standing in range(2, number_of + 1)]
    spare, counts = total - bound - (number_of - 1), [1] * (number_of - 1)
    while spare > 0:
        free = [i for i in range(number_of - 1) if counts[i] < bound]
        whole, remaining = sum([portions[i] for i in free]), spare
        for i in free:
            extra = min(bound - counts[i], max(1, remaining * portions[i] // whole), spare)
            counts[i] = counts[i] + extra
            spare = spare - extra
    return np.array([bound] + counts)


def ragged(rng, count, total, bound, lean):
    if count == 2:
        one = jax.random.randint(rng, (), max(1, total - bound), min(bound, total - 1) + 1)
        return jnp.stack([one, total - one])
    sizes = jnp.asarray(profile(count, total, bound, lean), jnp.int32)
    couples = (count - 1) // 2
    source_of, taker = sizes[1:1 + 2 * couples:2], sizes[2:2 + 2 * couples:2]
    margin = jnp.minimum(source_of - 1, bound - taker)
    passed = jax.random.randint(jax.random.fold_in(rng, 1), (couples,), 0, 1 << 20) % (margin + 1)
    sizes = sizes.at[1:1 + 2 * couples:2].set(source_of - passed).at[2:2 + 2 * couples:2].set(taker + passed)
    return sizes[jax.random.permutation(jax.random.fold_in(rng, 2), count)]


def assign_block(stream_key, own, number, rows, amount, top, limit, lean):
    sequence = jax.random.permutation(stream_key, amount)
    crowded, common = load_shares(amount, rows * top, limit, lean, True), load_shares(amount, rows * top, limit, lean, False)
    places = jnp.arange(amount)

    def named(sizes, offset_by):
        used = int((sizes > 0).sum())
        fixed = max(1, used // 4)
        passed = fixed + (places - fixed + offset_by * (used - fixed)) % max(1, amount - fixed)
        return jnp.zeros((amount,), jnp.int32).at[sequence[jnp.where(places < fixed, places, passed)]].set(jnp.asarray(sizes, jnp.int32))

    sizes = jnp.where(number % 4 == 0, named(crowded, number // 4), named(common, number - number // 4 - 1))
    mixed = jax.random.permutation(jax.random.fold_in(own, 3), amount)
    giver, receiver = mixed[0:amount // 2 * 2:2], mixed[1:amount // 2 * 2:2]
    margin = jnp.minimum(sizes[giver] - 1, limit - sizes[receiver]) // 2
    margin = jnp.where((giver == sequence[0]) | (receiver == sequence[0]) | (sizes[receiver] == 0), 0, jnp.maximum(margin, 0))
    passed = jax.random.randint(jax.random.fold_in(own, 4), (amount // 2,), 0, 1 << 20) % (margin + 1)
    sizes = sizes.at[giver].add(-passed).at[receiver].add(passed)
    labels = jnp.searchsorted(jnp.cumsum(sizes), jnp.arange(rows * top), side="right").astype(jnp.int32)
    table = labels.reshape(top, rows).T
    table = table[jax.random.permutation(jax.random.fold_in(own, 1), rows)]
    offset_by = jax.random.randint(jax.random.fold_in(own, 2), (rows, 1), 0, top)
    return jnp.take_along_axis(table, (jnp.arange(top)[None, :] + offset_by) % top, axis=1)


def load_shares(count, total, limit, lean, full):
    portions = [(1 << 20) // math.isqrt(rank ** lean) + 1 for rank in range(1, count + 1)]
    largest = limit if full else min(limit, max(-(-total // count), total * portions[0] // sum(portions)))
    least = 1 if total - largest >= count - 1 else 0
    given, rest = [largest] + [least] * (count - 1), total - largest - least * (count - 1)
    while rest > 0:
        movable = [i for i in range(1, count) if given[i] < largest] or [i for i in range(1, count) if given[i] < limit]
        pool, remaining = sum([portions[i] for i in movable]), rest
        for i in movable:
            addition = min(limit - given[i], max(1, remaining * portions[i] // pool), rest)
            given[i] = given[i] + addition
            rest = rest - addition
    return np.array(given)


def noise(key, dims, deviation, bound, pieces=(), kind=jnp.bfloat16):
    result = deviation * jax.random.normal(key, dims, jnp.float32)
    if pieces:
        result = result * shard_levels(key, dims, pieces, -0.22, 0.18)
    return jnp.clip(result, -bound, bound).astype(kind)


def setup_inputs(seed: int = 0) -> dict:
    key_list = jax.random.split(jax.random.key(seed), 10)
    columns = noise(key_list[0], (N_GRP, NL, FACES), 1.0, 6.0, ((0, 2), (2, 64)), jnp.float32)
    operators = draw_operators(jax.random.fold_in(key_list[9], 71), 0)
    normal_weights = noise(key_list[2], (2, NL), NL ** -0.5, 0.75, (), jnp.float32)
    face_patch_keys = jax.random.split(jax.random.fold_in(key_list[3], 1), FACES // S)
    face_patch_turns = jax.random.permutation(jax.random.fold_in(key_list[3], 3), FACES // S)
    face_patch = jax.vmap(lambda own, number: assign_block(jax.random.fold_in(key_list[3], 2), own, number, S, N_BLK, 1, CAP, 2))(face_patch_keys, face_patch_turns).reshape((FACES, 1))
    face_point = plant(jax.random.randint(key_list[4], (FACES,), 0, S), jax.random.fold_in(key_list[4], 1), 0, S - 1).astype(jnp.int32)
    live_count = ragged(key_list[5], N_BLK, S * N_BLK * 7 // 8, S, 2).astype(jnp.int32)
    impinged = plant((jax.random.randint(key_list[6], (FACES,), 0, 3) < 1).astype(jnp.int32), jax.random.fold_in(key_list[6], 1), 0, 1)
    crystal_load = jnp.clip(jnp.exp(math.log(2.0) - 2.3025851 * jax.random.uniform(key_list[7], (FACES,), jnp.float32) ** shard_levels(key_list[7], (FACES,), ((0, 64),), -0.2, 0.2)), 0.2, 2.0)
    film = jnp.clip(jnp.exp(math.log(1.0) - 2.9957323 * jax.random.uniform(key_list[8], (FACES,), jnp.float32) ** shard_levels(key_list[8], (FACES,), ((0, 64),), -0.2, 0.2)), 0.05, 1.0)
    return dict(columns=columns, operators=operators, normal_weights=normal_weights, face_patch=face_patch, face_point=face_point, live_count=live_count, impinged=impinged, crystal_load=crystal_load, film=film)


def lateral(row):
    padded = jnp.pad(row, 1)
    return padded[:-2] + padded[2:] - 2.0 * row


def reference(columns, operators, normal_weights, face_patch, face_point, live_count, impinged, crystal_load, film):
    faces = N_BLK * S
    highest = lax.Precision.HIGHEST
    order = jnp.arange(faces, dtype=jnp.int32)
    live = ((order % S) < jnp.repeat(live_count, S)).astype(jnp.float32)
    gas = columns[0]
    wall = columns[1]
    flux = (jnp.dot(normal_weights[0], gas, precision=highest, preferred_element_type=jnp.float32) + 0.25 * lateral(gas[0])) * live
    crystal = impinged.astype(jnp.float32) * crystal_load * live
    target = (face_patch[:, 0] * S + face_point).astype(jnp.int32)
    heat = jax.ops.segment_sum(flux, target, num_segments=faces)
    mass = jax.ops.segment_sum(crystal, target, num_segments=faces)
    for step in range(ITERS):
        source = 0.2 * (heat - 0.5 * mass + 0.5 * lateral(wall[0]))
        wall = jnp.dot(operators[1], wall.at[0].add(source), precision=highest, preferred_element_type=jnp.float32)
    film_new = jnp.maximum(film + 0.5 * (wall[0] - 0.3) - 0.1 * mass, 0.0)
    wall_surface = jnp.stack([wall[0], film_new])
    face_values = wall_surface[:, target] * live[None, :]
    gas_new = jnp.dot(operators[0], gas, precision=highest, preferred_element_type=jnp.float32) + normal_weights[1][:, None] * face_values[0][None, :]
    return jnp.stack([gas_new, wall]), jnp.stack([face_values, wall_surface])
```

```python
import jax
import jax.numpy as jnp
from jax import lax
from jax.experimental import pallas as pl
from jax.experimental.pallas import tpu as pltpu
from jax.sharding import PartitionSpec as P

ITERS = 4
L = 128
HALO = ITERS
ROWS = 12
FACE_CHUNK = 2048
SLOT_STEP = 8

f32 = jnp.float32
bf16 = jnp.bfloat16
i32 = jnp.int32
HIGHEST = lax.Precision.HIGHEST
NT = (((1,), (1,)), ((), ()))
NN = (((1,), (0,)), ((), ()))


def iota(shape, dim):
    return lax.broadcasted_iota(i32, shape, dim)


def split(x):
    high = x.astype(bf16).astype(f32)
    return high, x - high


def dot(a, b, dims=NN, precision=None):
    return lax.dot_general(a, b, dims, precision=precision, preferred_element_type=f32)


def onehot(mask):
    return jnp.where(mask, 1.0, 0.0).astype(bf16)


def masked(mask, x):
    return jnp.where(mask, x, 0.0).astype(bf16)


def route(width, blocks, capacity):
    c = FACE_CHUNK
    steps = width // c
    per = capacity // L
    highs = blocks * per
    sub = 256

    def kernel(live_ref, patch_ref, point_ref, v0_ref, side_ref, weight_ref, out_ref, slot_ref, carry, acc, eacc):
        i = pl.program_id(0)

        @pl.when(i == 0)
        def _():
            carry[...] = jnp.zeros_like(carry)
            acc[...] = jnp.zeros_like(acc)
            eacc[...] = jnp.zeros_like(eacc)

        patch, point = patch_ref[...], point_ref[...]
        named = iota((blocks, c), 0) == patch
        hot = onehot(named)
        upto = onehot(iota((sub, sub), 0) <= iota((sub, sub), 1))
        before = carry[...]
        ranks = []
        for j in range(c // sub):
            cut = slice(j * sub, (j + 1) * sub)
            count = dot(hot[:, cut], upto)
            ranks.append(jnp.sum(jnp.where(named[:, cut], count + before, 0.0), axis=0, keepdims=True))
            before = before + count[:, sub - 1 : sub]
        carry[...] = before
        rank = jnp.concatenate(ranks, axis=1).astype(i32) - 1
        slot = patch * capacity + rank
        slot_ref[...] = slot

        live = (iota((1, c), 1) + i * c) < live_ref[0]
        value = v0_ref[...] + jnp.sum(weight_ref[...] * side_ref[...], axis=0, keepdims=True)
        value = jnp.where(live, value, 0.0)
        v_high, v_low = split(value)
        t_high, t_low = ((point >> 7).astype(f32), (point & (L - 1)).astype(f32))
        high = onehot(iota((highs, c), 0) == (slot >> 7))
        low = iota((L, c), 0) == (slot & (L - 1))
        laid = jnp.concatenate([masked(low, x) for x in (v_high, v_low, t_high, t_low)], axis=0)
        placed = dot(high, laid, NT)
        for q in range(4):
            acc[pl.ds(q * highs, highs), :] += placed[:, q * L : (q + 1) * L]

        last = point >= width - 3
        edge_patch = jnp.where(last, patch + 1, jnp.where(point < 3, patch - 1, -1))
        edge_point = jnp.where(last, point - (width - 8), point)
        edge_hot = onehot(iota((blocks, c), 0) == edge_patch)
        edge_low = iota((8, c), 0) == edge_point
        zeros = jnp.zeros((L - 16, c), bf16)
        edges = jnp.concatenate([masked(edge_low, v_high), masked(edge_low, v_low)], axis=0)
        eacc[...] += dot(edge_hot, jnp.concatenate([edges, zeros], axis=0), NT)

        @pl.when(i == steps - 1)
        def _():
            for r in range(per):
                part = [acc[pl.ds(q * highs + r, blocks, stride=per), :] for q in range(4)]
                out_ref[pl.ds(r, blocks, stride=ROWS), :] = part[0] + part[1]
                out_ref[pl.ds(per + r, blocks, stride=ROWS), :] = part[2] * float(L) + part[3]
            edge = eacc[...]
            lane = iota(edge.shape, 1)
            both = edge + pltpu.roll(edge, L - 8, 1)
            out_ref[pl.ds(2 * per, blocks, stride=ROWS), :] = jnp.where(lane < 8, both, 0.0)
            for r in range(2 * per + 1, ROWS):
                out_ref[pl.ds(r, blocks, stride=ROWS), :] = jnp.zeros((blocks, L), f32)

    def call(live_count, patch, point, v0, side, weight):
        row = pl.BlockSpec((1, c), lambda i: (0, i))
        return pl.pallas_call(
            kernel,
            grid=(steps,),
            in_specs=[
                pl.BlockSpec(memory_space=pltpu.SMEM),
                row,
                row,
                row,
                pl.BlockSpec((side.shape[0], c), lambda i: (0, i)),
                pl.BlockSpec(weight.shape, lambda i: (0, 0)),
            ],
            out_specs=[pl.BlockSpec((blocks * ROWS, L), lambda i: (0, 0)), row],
            out_shape=[
                jax.ShapeDtypeStruct((blocks * ROWS, L), f32),
                jax.ShapeDtypeStruct((1, width), i32),
            ],
            scratch_shapes=[
                pltpu.VMEM((blocks, 1), f32),
                pltpu.VMEM((4 * highs, L), f32),
                pltpu.VMEM((blocks, L), f32),
            ],
            name="route",
        )(live_count, patch, point, v0, side, weight)

    return call


def matrices(nl, width):
    c = FACE_CHUNK
    steps = width // c
    out_rows = nl + 8
    tail = (ITERS + 1) * width // L

    def kernel(flag_ref, op_ref, weight_ref, halo_ref, side_ref, y_ref, rows_ref, coef_ref, lhs):
        i = pl.program_id(0)

        @pl.when(i == 0)
        def _():
            gas = flag_ref[0] == 1
            one = op_ref[...]
            two = dot(one, one, precision=HIGHEST)
            three = dot(two, one, precision=HIGHEST)
            four = dot(two, two, precision=HIGHEST)
            main = jnp.where(gas, one, four)
            unit = jnp.where(iota((1, nl), 1) == 0, 1.0, 0.0)
            full = jnp.concatenate([main, unit, one[0:1], two[0:1], three[0:1], four[0:1], jnp.zeros((3, nl), f32)], axis=0)
            high, low = split(full)
            lhs[...] = jnp.concatenate([high, low, high, low], axis=1).astype(bf16)
            rows_ref[pl.ds(tail, 8), :] = dot(full[nl:], halo_ref[...], precision=HIGHEST)
            lead = [jnp.broadcast_to(m[0:1, 0:1], (1, L)) for m in (one, two, three, four)]
            rows_ref[pl.ds(tail + 8, 8), :] = jnp.concatenate(lead + [jnp.zeros((4, L), f32)], axis=0)
            lane = iota((nl, L), 1)
            coef = jnp.where(lane == 0, jnp.where(gas, weight_ref[...], four[:, 0:1]), 0.0)
            for k, m in ((1, three), (2, two), (3, one)):
                coef = jnp.where(lane == k, jnp.where(gas, 0.0, m[:, 0:1]), coef)
            coef_ref[...] = coef

        high, low = split(side_ref[...])
        high, low = high.astype(bf16), low.astype(bf16)
        out = dot(lhs[...], jnp.concatenate([high, high, low, low], axis=0))
        y_ref[...] = out[:nl]
        for n in range(ITERS + 1):
            part = [out[nl + n : nl + n + 1, k * L : (k + 1) * L] for k in range(c // L)]
            start = pl.multiple_of(n * (width // L) + i * (c // L), 8)
            rows_ref[pl.ds(start, c // L), :] = jnp.concatenate(part, axis=0)

    def call(flag, op, weight, halo, side):
        return pl.pallas_call(
            kernel,
            grid=(steps,),
            in_specs=[
                pl.BlockSpec(memory_space=pltpu.SMEM),
                pl.BlockSpec((nl, nl), lambda i: (0, 0)),
                pl.BlockSpec((nl, 1), lambda i: (0, 0)),
                pl.BlockSpec((nl, L), lambda i: (0, 0)),
                pl.BlockSpec((nl, c), lambda i: (0, i)),
            ],
            out_specs=[
                pl.BlockSpec((nl, c), lambda i: (0, i)),
                pl.BlockSpec((tail + 16, L), lambda i: (0, 0)),
                pl.BlockSpec((nl, L), lambda i: (0, 0)),
            ],
            out_shape=[
                jax.ShapeDtypeStruct((nl, width), f32),
                jax.ShapeDtypeStruct((tail + 16, L), f32),
                jax.ShapeDtypeStruct((nl, L), f32),
            ],
            scratch_shapes=[pltpu.VMEM((out_rows, 4 * nl), bf16)],
            name="matrices",
        )(flag, op, weight, halo, side)

    return call


def gather_sum(width, blocks, capacity):
    per = capacity // L
    tall = width // L

    def kernel(x_ref, out_ref, acc):
        acc[...] = jnp.zeros_like(acc)

        def step(s, edge):
            start = pl.multiple_of(s * SLOT_STEP * ROWS, 8)
            x = x_ref[pl.ds(start, SLOT_STEP * ROWS), :]
            v_high, v_low = split(x)
            t = x.astype(i32)
            t_high, t_low = t >> 7, t & (L - 1)
            highs, lows = [], []
            for m in range(SLOT_STEP):
                edge = edge + x[m * ROWS + 2 * per : m * ROWS + 2 * per + 1]
                for r in range(per):
                    a, b = m * ROWS + r, m * ROWS + per + r
                    highs.append(onehot(iota((tall, L), 0) == t_high[b : b + 1]))
                    low = iota((L, L), 0) == t_low[b : b + 1]
                    lows.append(jnp.concatenate([masked(low, v_high[a : a + 1]), masked(low, v_low[a : a + 1])], axis=0))
            acc[...] += dot(jnp.concatenate(highs, axis=1), jnp.concatenate(lows, axis=1), NT)
            return edge

        edge = lax.fori_loop(0, blocks // SLOT_STEP, step, jnp.zeros((1, L), f32))
        out_ref[pl.ds(0, tall), :] = acc[:, :L] + acc[:, L:]
        out_ref[pl.ds(tall, 8), :] = jnp.broadcast_to(edge, (8, L))

    def call(x):
        return pl.pallas_call(
            kernel,
            out_shape=jax.ShapeDtypeStruct((tall + 8, L), f32),
            scratch_shapes=[pltpu.VMEM((tall, 2 * L), f32)],
            name="gather_sum",
        )(x)

    return call


def surface_lookup(width, blocks, capacity):
    per = capacity // L
    tall = width // L
    ext = tall + 16

    def kernel(flag_ref, mine_ref, other_ref, rows_ref, film_ref, x_ref, out_ref, source_ref, surface_ref):
        gas = flag_ref[0] == 1
        lane, line = iota((ext, L), 1), iota((ext, L), 0)
        inside = (line >= 8) & (line < tall + 8)
        left = (line == 7) & (lane >= L - HALO)
        right = (line == tall + 8) & (lane < HALO)
        valid = inside | (left & (flag_ref[1] == 1)) | (right & (flag_ref[2] == 1))

        def extend(body, edge_left, edge_right):
            zeros = jnp.zeros((7, L), f32)
            full = jnp.concatenate([zeros, edge_left, body, edge_right, zeros], axis=0)
            return jnp.where(valid, full, 0.0)

        def lateral(x):
            ahead = pltpu.roll(x, L - 1, 1)
            ahead = jnp.where(lane == L - 1, pltpu.roll(ahead, ext - 1, 0), ahead)
            behind = pltpu.roll(x, 1, 1)
            behind = jnp.where(lane == 0, pltpu.roll(behind, 1, 0), behind)
            return behind + ahead - 2.0 * x

        mine, other = mine_ref[...], other_ref[...]
        heat, mass = jnp.where(gas, mine, other), jnp.where(gas, other, mine)
        q = heat - 0.5 * mass
        q_edge = q[tall : tall + 1]
        q = extend(q[:tall], pltpu.roll(q_edge, L - 8, 1), q_edge)
        tail = (ITERS + 1) * tall
        lead = rows_ref[pl.ds(tail + 8, 8), :]

        def base(n):
            edge = rows_ref[pl.ds(tail + n, 1), :]
            return extend(rows_ref[pl.ds(n * tall, tall), :], edge, edge)

        sources = []
        row = base(0)
        for n in range(1, ITERS + 1):
            sources.append(0.2 * (q + 0.5 * lateral(row)))
            row = base(n)
            for j, source in enumerate(sources):
                row = row + lead[n - 1 - j : n - j] * source
            row = jnp.where(valid, row, 0.0)
        for n in range(ITERS):
            source_ref[pl.ds(n * tall, tall), :] = sources[n][8 : tall + 8]
        wall_row = row[8 : tall + 8]
        film_new = jnp.maximum(film_ref[...] + 0.5 * (wall_row - 0.3) - 0.1 * mass[:tall], 0.0)
        surface_ref[pl.ds(0, tall), :] = wall_row
        surface_ref[pl.ds(tall, tall), :] = film_new

        high, low = split(jnp.where(gas, film_new, wall_row).T)
        table = jnp.concatenate([high, low], axis=1).astype(bf16)

        def step(s, carry):
            start = pl.multiple_of(s * SLOT_STEP * ROWS, 8)
            t = x_ref[pl.ds(start, SLOT_STEP * ROWS), :].astype(i32)
            t_high, t_low = t >> 7, t & (L - 1)
            rows = [m * ROWS + per + r for m in range(SLOT_STEP) for r in range(per)]
            highs = jnp.concatenate([onehot(iota((tall, L), 0) == t_high[b : b + 1]) for b in rows], axis=1)
            found = dot(table, jnp.concatenate([highs, highs], axis=0))
            picked = []
            for k, b in enumerate(rows):
                low = iota((L, L), 0) == t_low[b : b + 1]
                picked.append(jnp.sum(jnp.where(low, found[:, k * L : (k + 1) * L], 0.0), axis=0, keepdims=True))
            size = SLOT_STEP * per
            out_ref[pl.ds(pl.multiple_of(s * size, 8), size), :] = jnp.concatenate(picked, axis=0)
            return carry

        lax.fori_loop(0, blocks // SLOT_STEP, step, 0)

    def call(flags, mine, other, rows, film, x):
        vmem = pl.BlockSpec(memory_space=pltpu.VMEM)
        return pl.pallas_call(
            kernel,
            in_specs=[pl.BlockSpec(memory_space=pltpu.SMEM)] + [vmem] * 5,
            out_shape=[
                jax.ShapeDtypeStruct((blocks * per, L), f32),
                jax.ShapeDtypeStruct((ITERS * tall, L), f32),
                jax.ShapeDtypeStruct((2 * tall, L), f32),
            ],
            name="surface_lookup",
        )(flags, mine, other, rows, film, x)

    return call


def face_lookup(width, blocks, capacity):
    c = FACE_CHUNK
    steps = width // c
    highs = blocks * capacity // L

    def kernel(live_ref, reply_ref, slot_ref, out_ref, table):
        i = pl.program_id(0)

        @pl.when(i == 0)
        def _():
            high, low = split(reply_ref[...].T)
            table[...] = jnp.concatenate([high, low], axis=1).astype(bf16)

        slot = slot_ref[...]
        hot = onehot(iota((highs, c), 0) == (slot >> 7))
        found = dot(table[...], jnp.concatenate([hot, hot], axis=0))
        low = iota((L, c), 0) == (slot & (L - 1))
        live = (iota((1, c), 1) + i * c) < live_ref[0]
        picked = jnp.where(live, jnp.sum(jnp.where(low, found, 0.0), axis=0, keepdims=True), 0.0)
        out_ref[...] = jnp.concatenate([picked[:, k * L : (k + 1) * L] for k in range(c // L)], axis=0)

    def call(live_count, reply, slot):
        return pl.pallas_call(
            kernel,
            grid=(steps,),
            in_specs=[
                pl.BlockSpec(memory_space=pltpu.SMEM),
                pl.BlockSpec((highs, L), lambda i: (0, 0)),
                pl.BlockSpec((1, c), lambda i: (0, i)),
            ],
            out_specs=pl.BlockSpec((c // L, L), lambda i: (i, 0)),
            out_shape=jax.ShapeDtypeStruct((width // L, L), f32),
            scratch_shapes=[pltpu.VMEM((L, 2 * highs), bf16)],
            name="face_lookup",
        )(live_count, reply, slot)

    return call


def finish(nl, width):
    c = FACE_CHUNK
    steps = width // c
    tall = width // L
    part = c // L

    def kernel(flag_ref, y_ref, coef_ref, source_ref, surface_ref, mine_ref, other_ref, out_ref, rows_ref):
        gas = flag_ref[0] == 1
        film, first = mine_ref[...], other_ref[...]
        coef = coef_ref[...]
        sources = [jnp.where(gas, first, source_ref[0])] + [source_ref[n] for n in range(1, ITERS)]
        spread = [jnp.broadcast_to(coef[:, n : n + 1], (nl, L)) for n in range(ITERS)]
        for k in range(part):
            cut = slice(k * L, (k + 1) * L)
            total = y_ref[:, cut]
            for n in range(ITERS):
                total = total + spread[n] * sources[n][k : k + 1]
            out_ref[:, cut] = total
        top = jnp.where(gas, first, surface_ref[0])
        bottom = jnp.where(gas, film, surface_ref[1])
        for n, x in enumerate((top, bottom)):
            rows_ref[n : n + 1, :] = jnp.concatenate([x[k : k + 1] for k in range(part)], axis=1)

    def call(flag, y, coef, source, surface, mine, other):
        tile = pl.BlockSpec((part, L), lambda i: (i, 0))
        return pl.pallas_call(
            kernel,
            grid=(steps,),
            in_specs=[
                pl.BlockSpec(memory_space=pltpu.SMEM),
                pl.BlockSpec((nl, c), lambda i: (0, i)),
                pl.BlockSpec((nl, L), lambda i: (0, 0)),
                pl.BlockSpec((ITERS, part, L), lambda i: (0, i, 0)),
                pl.BlockSpec((2, part, L), lambda i: (0, i, 0)),
                tile,
                tile,
            ],
            out_specs=[pl.BlockSpec((nl, c), lambda i: (0, i)), pl.BlockSpec((2, c), lambda i: (0, i))],
            out_shape=[jax.ShapeDtypeStruct((nl, width), f32), jax.ShapeDtypeStruct((2, width), f32)],
            name="finish",
        )(flag, y, coef, source.reshape(ITERS, tall, L), surface.reshape(2, tall, L), mine, other)

    return call


def local(columns, operators, normal_weights, face_patch, face_point, live_count, impinged, crystal_load, film):
    nl, width = columns.shape[1:]
    blocks = lax.axis_size("blk")
    capacity = 2 * width // blocks
    per = capacity // L
    tall = width // L
    block = lax.axis_index("blk")
    gas = lax.axis_index("grp") == 0
    side, matrix = columns[0], operators[0]
    flags = jnp.stack([gas, block > 0, block < blocks - 1]).astype(i32)

    up = [(i, i + 1) for i in range(blocks - 1)]
    down = [(i + 1, i) for i in range(blocks - 1)]
    swap = [(i, blocks + i) for i in range(blocks)] + [(blocks + i, i) for i in range(blocks)]
    left = lax.ppermute(side[:, width - HALO :], "blk", up)
    right = lax.ppermute(side[:, :HALO], "blk", down)
    halo = jnp.concatenate([right, jnp.zeros((nl, L - 2 * HALO), f32), left], axis=1)

    row = side[0]
    before = jnp.concatenate([jnp.zeros((1,), f32), row[:-1]])
    after = jnp.concatenate([row[1:], jnp.zeros((1,), f32)])
    v0 = jnp.where(gas, 0.25 * (before + after - 2.0 * row), impinged.astype(f32) * crystal_load)
    weight = jnp.where(gas, normal_weights[0], 0.0)[:, None]
    patch, point = face_patch.reshape(1, width), face_point.reshape(1, width)
    message, slot = route(width, blocks, capacity)(live_count, patch, point, v0.reshape(1, width), side, weight)

    lines, lanes = lax.broadcasted_iota(i32, message.shape, 0), lax.broadcasted_iota(i32, message.shape, 1)
    for f, amount in ((0, left[0, HALO - 1]), (width - 1, right[0, 0])):
        amount = jnp.where(gas & (live_count[0] > f), 0.25 * amount, 0.0)
        where, name, spot = slot[0, f], patch[0, f], point[0, f]
        line = (where // capacity) * ROWS + (where // L) % per
        message = message + jnp.where((lines == line) & (lanes == where % L), amount, 0.0)
        last = spot >= width - 3
        edge = jnp.where(last, name + 1, jnp.where(spot < 3, name - 1, -1))
        at = jnp.where(last, spot - (width - 8), spot)
        line = jnp.where(edge < 0, -1, edge * ROWS + 2 * per)
        message = message + jnp.where((lines == line) & (lanes == at), amount, 0.0)

    arrived = lax.all_to_all(message.reshape(-1), "blk", split_axis=0, concat_axis=0, tiled=True)
    arrived = arrived.reshape(blocks * ROWS, L)
    y, rows, coef = matrices(nl, width)(flags, matrix, normal_weights[1][:, None], halo, side)
    swapped = lax.ppermute(rows, ("grp", "blk"), swap)
    rows = jnp.where(gas, swapped, rows)

    mine = gather_sum(width, blocks, capacity)(arrived)
    other = lax.ppermute(mine, ("grp", "blk"), swap)
    replies, source, surface = surface_lookup(width, blocks, capacity)(flags, mine, other, rows, film.reshape(tall, L), arrived)
    returned = lax.all_to_all(replies.reshape(-1), "blk", split_axis=0, concat_axis=0, tiled=True)
    found = face_lookup(width, blocks, capacity)(live_count, returned.reshape(blocks * per, L), slot)
    paired = lax.ppermute(found, ("grp", "blk"), swap)
    new_columns, surface = finish(nl, width)(flags, y, coef, source, surface, found, paired)
    return new_columns[None], surface[None]


def solution(mesh):
    return jax.shard_map(
        local,
        mesh=mesh,
        in_specs=(
            P("grp", None, "blk"),
            P("grp", None, None),
            P(),
            P("blk", None),
            P("blk"),
            P("blk"),
            P("blk"),
            P("blk"),
            P("blk"),
        ),
        out_specs=(P("grp", None, "blk"), P("grp", None, "blk")),
        check_vma=False,
    )
```

```python
import jax
import jax.numpy as jnp
from jax import lax
from jax.experimental import pallas as pl
from jax.experimental.pallas import tpu as pltpu
from jax.sharding import PartitionSpec as P

ITERS = 4
L = 128
HALO = ITERS
ROWS = 12
FACE_CHUNK = 2048
SLOT_STEP = 8

f32 = jnp.float32
bf16 = jnp.bfloat16
i32 = jnp.int32
HIGHEST = lax.Precision.HIGHEST
NT = (((1,), (1,)), ((), ()))
NN = (((1,), (0,)), ((), ()))


def iota(shape, dim):
    return lax.broadcasted_iota(i32, shape, dim)


def split(x):
    high = x.astype(bf16).astype(f32)
    return high, x - high


def dot(a, b, dims=NN, precision=None):
    return lax.dot_general(a, b, dims, precision=precision, preferred_element_type=f32)


def onehot(mask):
    return jnp.where(mask, 1.0, 0.0).astype(bf16)


def masked(mask, x):
    return jnp.where(mask, x, 0.0).astype(bf16)


def transposed(x):
    m, n = x.shape
    if n < L:
        x = jnp.concatenate([x, jnp.zeros((m, L - n), f32)], axis=1)
    if m < L:
        x = jnp.concatenate([x, jnp.zeros((L - m, L), f32)], axis=0)
    return x.T


def edge_of(patch, point, width):
    last = point >= width - 3
    return (
        jnp.where(last, patch + 1, jnp.where(point < 3, patch - 1, -1)),
        jnp.where(last, point - (width - 8), point),
    )


def route(width, blocks, capacity):
    c = FACE_CHUNK
    steps = width // c
    per = capacity // L
    highs = blocks * per
    sub = 256

    def kernel(
        live_ref,
        patch_ref,
        point_ref,
        impinged_ref,
        load_ref,
        side_ref,
        before_ref,
        after_ref,
        weight_ref,
        out_ref,
        slot_ref,
        carry,
        acc,
        eacc,
        weight,
        first_face,
        first_side,
    ):
        i = pl.program_id(0)
        gas = lax.axis_index("grp") == 0
        patch, point, side = patch_ref[...], point_ref[...], side_ref[...]

        @pl.when(i == 0)
        def _():
            carry[...] = jnp.zeros_like(carry)
            acc[...] = jnp.zeros_like(acc)
            eacc[...] = jnp.zeros_like(eacc)
            nl = side.shape[0]
            weight[...] = transposed(weight_ref[...])[:nl]
            first_face[0:1, :] = patch[:, :L]
            first_face[1:2, :] = point[:, :L]
            first_side[...] = side[:, :L]

        named = iota((blocks, c), 0) == patch
        hot = onehot(named)
        upto = onehot(iota((sub, sub), 0) <= iota((sub, sub), 1))
        before = carry[...]
        ranks = []
        for j in range(c // sub):
            cut = slice(j * sub, (j + 1) * sub)
            count = dot(hot[:, cut], upto)
            ranks.append(jnp.sum(jnp.where(named[:, cut], count + before, 0.0), axis=0, keepdims=True))
            before = before + count[:, sub - 1 : sub]
        carry[...] = before
        rank = jnp.concatenate(ranks, axis=1).astype(i32) - 1
        slot = patch * capacity + rank
        slot_ref[...] = slot

        lane = iota((1, c), 1)
        live = (lane + i * c) < live_ref[0]
        row = side[0:1]
        ahead = jnp.where(lane == c - 1, jnp.where(i == steps - 1, 0.0, after_ref[0:1, 0:1]), pltpu.roll(row, c - 1, 1))
        behind = jnp.where(lane == 0, jnp.where(i == 0, 0.0, before_ref[0:1, L - 1 : L]), pltpu.roll(row, 1, 1))
        flux = jnp.sum(weight[:, 0:1] * side, axis=0, keepdims=True) + 0.25 * (behind + ahead - 2.0 * row)
        crystal = impinged_ref[...].astype(f32) * load_ref[...]
        value = jnp.where(live, jnp.where(gas, flux, crystal), 0.0)
        v_high, v_low = split(value)
        t_high, t_low = ((point >> 7).astype(f32), (point & (L - 1)).astype(f32))
        high = onehot(iota((highs, c), 0) == (slot >> 7))
        low = iota((L, c), 0) == (slot & (L - 1))
        laid = jnp.concatenate([masked(low, x) for x in (v_high, v_low, t_high, t_low)], axis=0)
        placed = dot(high, laid, NT)
        for q in range(4):
            acc[pl.ds(q * highs, highs), :] += placed[:, q * L : (q + 1) * L]

        edge_patch, edge_point = edge_of(patch, point, width)
        edge_hot = onehot(iota((blocks, c), 0) == edge_patch)
        edge_low = iota((8, c), 0) == edge_point
        zeros = jnp.zeros((L - 16, c), bf16)
        edges = jnp.concatenate([masked(edge_low, v_high), masked(edge_low, v_low)], axis=0)
        eacc[...] += dot(edge_hot, jnp.concatenate([edges, zeros], axis=0), NT)

        @pl.when(i == steps - 1)
        def _():
            for r in range(per):
                part = [acc[pl.ds(q * highs + r, blocks, stride=per), :] for q in range(4)]
                out_ref[pl.ds(r, blocks, stride=ROWS), :] = part[0] + part[1]
                out_ref[pl.ds(per + r, blocks, stride=ROWS), :] = part[2] * float(L) + part[3]
            edge = eacc[...]
            spot, to = iota(edge.shape, 1), iota(edge.shape, 0)
            info = jnp.where(spot < 8, edge + pltpu.roll(edge, L - 8, 1), 0.0)
            info = jnp.where((spot == 8) & gas, first_side[0:1, 0:1], info)
            info = jnp.where((spot == 9) & gas, row[:, c - 1 :], info)
            ends = (
                (10, first_face[0:1, 0:1], first_face[1:2, 0:1], live_ref[0] > 0),
                (11, patch[:, c - 1 :], point[:, c - 1 :], live_ref[0] >= width),
            )
            for at, name, target, alive in ends:
                info = jnp.where(spot == at, jnp.where((to == name) & alive, target.astype(f32), -1.0), info)
                name, target = edge_of(name, target, width)
                info = jnp.where(spot == at + 2, jnp.where((to == name) & alive, target.astype(f32), -1.0), info)
            out_ref[pl.ds(2 * per, blocks, stride=ROWS), :] = info
            block = lax.axis_index("blk")
            half = spot[:1] < L // 2
            left, right = transposed(first_side[...]), transposed(side[:, c - L :])
            for r in range(2):
                rows = []
                for ends, base in ((left, 0), (right, L - HALO)):
                    j = base + 2 * r
                    rows.append(jnp.where(half, ends[j : j + 1], pltpu.roll(ends[j + 1 : j + 2], L // 2, 1)))
                sent = jnp.where(to == block - 1, rows[0], jnp.where(to == block + 1, rows[1], 0.0))
                out_ref[pl.ds(2 * per + 1 + r, blocks, stride=ROWS), :] = sent
            for r in range(2 * per + 3, ROWS):
                out_ref[pl.ds(r, blocks, stride=ROWS), :] = jnp.zeros((blocks, L), f32)

    def call(live_count, patch, point, impinged, load, side, weights):
        nl = side.shape[0]
        row = pl.BlockSpec((1, c), lambda i: (0, i))
        return pl.pallas_call(
            kernel,
            grid=(steps,),
            in_specs=[
                pl.BlockSpec(memory_space=pltpu.SMEM),
                row,
                row,
                row,
                row,
                pl.BlockSpec((nl, c), lambda i: (0, i)),
                pl.BlockSpec((8, L), lambda i: (0, jnp.maximum(i * (c // L) - 1, 0))),
                pl.BlockSpec((8, L), lambda i: (0, jnp.minimum((i + 1) * (c // L), width // L - 1))),
                pl.BlockSpec(weights.shape, lambda i: (0, 0)),
            ],
            out_specs=[pl.BlockSpec((blocks * ROWS, L), lambda i: (0, 0)), row],
            out_shape=[
                jax.ShapeDtypeStruct((blocks * ROWS, L), f32),
                jax.ShapeDtypeStruct((1, width), i32),
            ],
            scratch_shapes=[
                pltpu.VMEM((blocks, 1), f32),
                pltpu.VMEM((4 * highs, L), f32),
                pltpu.VMEM((blocks, L), f32),
                pltpu.VMEM((nl, L), f32),
                pltpu.VMEM((8, L), i32),
                pltpu.VMEM((nl, L), f32),
            ],
            name="route",
        )(live_count, patch, point, impinged, load, side, side, side, weights)

    return call


def matrices(nl, width):
    c = FACE_CHUNK
    steps = width // c
    out_rows = nl + 8
    tail = (ITERS + 1) * width // L

    def kernel(op_ref, weight_ref, side_ref, y_ref, rows_ref, coef_ref, lhs):
        i = pl.program_id(0)

        @pl.when(i == 0)
        def _():
            gas = lax.axis_index("grp") == 0
            coupling = transposed(weight_ref[...])[:nl, 1:2]
            one = op_ref[...]
            two = dot(one, one, precision=HIGHEST)
            three = dot(two, one, precision=HIGHEST)
            four = dot(two, two, precision=HIGHEST)
            main = jnp.where(gas, one, four)
            unit = jnp.where(iota((1, nl), 1) == 0, 1.0, 0.0)
            full = jnp.concatenate([main, unit, one[0:1], two[0:1], three[0:1], four[0:1], jnp.zeros((3, nl), f32)], axis=0)
            high, low = split(full)
            lhs[...] = jnp.concatenate([high, low, high, low], axis=1).astype(bf16)
            rows_ref[pl.ds(tail, 8), :] = jnp.concatenate([full[nl:], jnp.zeros((8, L - nl), f32)], axis=1)
            lead = [jnp.broadcast_to(m[0:1, 0:1], (1, L)) for m in (one, two, three, four)]
            rows_ref[pl.ds(tail + 8, 8), :] = jnp.concatenate(lead + [jnp.zeros((4, L), f32)], axis=0)
            lane = iota((nl, L), 1)
            coef = jnp.where(lane == 0, jnp.where(gas, coupling, four[:, 0:1]), 0.0)
            for k, m in ((1, three), (2, two), (3, one)):
                coef = jnp.where(lane == k, jnp.where(gas, 0.0, m[:, 0:1]), coef)
            coef_ref[...] = coef

        high, low = split(side_ref[...])
        high, low = high.astype(bf16), low.astype(bf16)
        out = dot(lhs[...], jnp.concatenate([high, high, low, low], axis=0))
        y_ref[...] = out[:nl]
        for n in range(ITERS + 1):
            part = [out[nl + n : nl + n + 1, k * L : (k + 1) * L] for k in range(c // L)]
            start = pl.multiple_of(n * (width // L) + i * (c // L), 8)
            rows_ref[pl.ds(start, c // L), :] = jnp.concatenate(part, axis=0)

    def call(op, weights, side):
        return pl.pallas_call(
            kernel,
            grid=(steps,),
            in_specs=[
                pl.BlockSpec((nl, nl), lambda i: (0, 0)),
                pl.BlockSpec(weights.shape, lambda i: (0, 0)),
                pl.BlockSpec((nl, c), lambda i: (0, i)),
            ],
            out_specs=[
                pl.BlockSpec((nl, c), lambda i: (0, i)),
                pl.BlockSpec((tail + 16, L), lambda i: (0, 0)),
                pl.BlockSpec((nl, L), lambda i: (0, 0)),
            ],
            out_shape=[
                jax.ShapeDtypeStruct((nl, width), f32),
                jax.ShapeDtypeStruct((tail + 16, L), f32),
                jax.ShapeDtypeStruct((nl, L), f32),
            ],
            scratch_shapes=[pltpu.VMEM((out_rows, 4 * nl), bf16)],
            name="matrices",
        )(op, weights, side)

    return call


def gather_sum(width, blocks, capacity):
    per = capacity // L
    tall = width // L

    def kernel(x_ref, out_ref, acc):
        def step(s, nothing):
            start = pl.multiple_of(s * SLOT_STEP * ROWS, 8)
            x = x_ref[pl.ds(start, SLOT_STEP * ROWS), :]
            v_high, v_low = split(x)
            t = x.astype(i32)
            t_high, t_low = t >> 7, t & (L - 1)
            highs, lows = [], []
            for m in range(SLOT_STEP):
                for r in range(per):
                    a, b = m * ROWS + r, m * ROWS + per + r
                    highs.append(onehot(iota((tall, L), 0) == t_high[b : b + 1]))
                    low = iota((L, L), 0) == t_low[b : b + 1]
                    lows.append(jnp.concatenate([masked(low, v_high[a : a + 1]), masked(low, v_low[a : a + 1])], axis=0))
            acc[...] += dot(jnp.concatenate(highs, axis=1), jnp.concatenate(lows, axis=1), NT)
            return nothing

        info = x_ref[pl.ds(2 * per, blocks, stride=ROWS), :]
        across = transposed(info)
        lane = iota((1, L), 1)
        left = lane < blocks

        def ends(a, b):
            return jnp.where(left, a, pltpu.roll(b, blocks, 1))

        value = 0.25 * ends(pltpu.roll(across[9:10], 1, 1), pltpu.roll(across[8:9], L - 1, 1))
        target = ends(across[10:11], across[11:12]).astype(i32)
        halo = ends(across[12:13], across[13:14]).astype(i32)
        v_high, v_low = split(value)
        low = iota((L, L), 0) == (target & (L - 1))
        high = onehot(iota((tall, L), 0) == (target >> 7))
        acc[...] = dot(high, jnp.concatenate([masked(low, v_high), masked(low, v_low)], axis=0), NT)
        at = onehot(iota((L, L), 0) == halo)
        pieces = jnp.concatenate([v_high, v_low, jnp.zeros((6, L), f32)], axis=0).astype(bf16)
        edge = jnp.sum(dot(pieces, at, NT), axis=0, keepdims=True)
        edge = edge + jnp.where(lane < 8, jnp.sum(info, axis=0, keepdims=True), 0.0)

        lax.fori_loop(0, blocks // SLOT_STEP, step, 0)
        out_ref[pl.ds(0, tall), :] = acc[:, :L] + acc[:, L:]
        block, source = lax.axis_index("blk"), iota((blocks, L), 0)
        rows = [edge]
        for near in (block - 1, block + 1):
            for r in range(2):
                columns = x_ref[pl.ds(2 * per + 1 + r, blocks, stride=ROWS), :]
                rows.append(jnp.sum(jnp.where(source == near, columns, 0.0), axis=0, keepdims=True))
        out_ref[pl.ds(tall, 8), :] = jnp.concatenate(rows + [jnp.zeros((3, L), f32)], axis=0)

    def call(x):
        return pl.pallas_call(
            kernel,
            out_shape=jax.ShapeDtypeStruct((tall + 8, L), f32),
            scratch_shapes=[pltpu.VMEM((tall, 2 * L), f32)],
            name="gather_sum",
        )(x)

    return call


def surface_lookup(width, blocks, capacity):
    per = capacity // L
    tall = width // L
    ext = tall + 16

    def kernel(mine_ref, other_ref, rows_ref, film_ref, x_ref, out_ref, source_ref, surface_ref):
        gas = lax.axis_index("grp") == 0
        block = lax.axis_index("blk")
        lane, line = iota((ext, L), 1), iota((ext, L), 0)
        inside = (line >= 8) & (line < tall + 8)
        left = (line == 7) & (lane >= L - HALO)
        right = (line == tall + 8) & (lane < HALO)
        valid = inside | (left & (block > 0)) | (right & (block < blocks - 1))

        def extend(body, edge_left, edge_right):
            zeros = jnp.zeros((7, L), f32)
            full = jnp.concatenate([zeros, edge_left, body, edge_right, zeros], axis=0)
            return jnp.where(valid, full, 0.0)

        def lateral(x):
            ahead = pltpu.roll(x, L - 1, 1)
            ahead = jnp.where(lane == L - 1, pltpu.roll(ahead, ext - 1, 0), ahead)
            behind = pltpu.roll(x, 1, 1)
            behind = jnp.where(lane == 0, pltpu.roll(behind, 1, 0), behind)
            return behind + ahead - 2.0 * x

        mine, other = mine_ref[...], other_ref[...]
        heat, mass = jnp.where(gas, mine, other), jnp.where(gas, other, mine)
        q = heat - 0.5 * mass
        q_edge = q[tall : tall + 1]
        q = extend(q[:tall], pltpu.roll(q_edge, L - 8, 1), q_edge)
        tail = (ITERS + 1) * tall
        lead = rows_ref[pl.ds(tail + 8, 8), :]
        near = jnp.where(gas, other[tall:], mine[tall:])
        half = lane[:1] < L // 2

        def columns(a):
            for x in (near[a : a + 1], near[a + 1 : a + 2]):
                yield jnp.where(half, x, 0.0)
                yield jnp.where(half, pltpu.roll(x, L // 2, 1), 0.0)

        gap = jnp.zeros((L - 2 * HALO, L), f32)
        halo = jnp.concatenate([*columns(3), gap, *columns(1)], axis=0)
        halo = dot(rows_ref[pl.ds(tail, 8), :], halo, NT, precision=HIGHEST)

        def base(n):
            edge = halo[n : n + 1]
            return extend(rows_ref[pl.ds(n * tall, tall), :], edge, edge)

        sources = []
        row = base(0)
        for n in range(1, ITERS + 1):
            sources.append(0.2 * (q + 0.5 * lateral(row)))
            row = base(n)
            for j, source in enumerate(sources):
                row = row + lead[n - 1 - j : n - j] * source
            row = jnp.where(valid, row, 0.0)
        for n in range(ITERS):
            source_ref[pl.ds(n * tall, tall), :] = sources[n][8 : tall + 8]
        wall_row = row[8 : tall + 8]
        film_new = jnp.maximum(film_ref[...] + 0.5 * (wall_row - 0.3) - 0.1 * mass[:tall], 0.0)
        surface_ref[pl.ds(0, tall), :] = wall_row
        surface_ref[pl.ds(tall, tall), :] = film_new

        high, low = split(jnp.where(gas, wall_row, film_new).T)
        table = jnp.concatenate([high, low], axis=1).astype(bf16)

        def step(s, carry):
            start = pl.multiple_of(s * SLOT_STEP * ROWS, 8)
            t = x_ref[pl.ds(start, SLOT_STEP * ROWS), :].astype(i32)
            t_high, t_low = t >> 7, t & (L - 1)
            rows = [m * ROWS + per + r for m in range(SLOT_STEP) for r in range(per)]
            highs = jnp.concatenate([onehot(iota((tall, L), 0) == t_high[b : b + 1]) for b in rows], axis=1)
            found = dot(table, jnp.concatenate([highs, highs], axis=0))
            picked = []
            for k, b in enumerate(rows):
                low = iota((L, L), 0) == t_low[b : b + 1]
                picked.append(jnp.sum(jnp.where(low, found[:, k * L : (k + 1) * L], 0.0), axis=0, keepdims=True))
            size = SLOT_STEP * per
            out_ref[pl.ds(pl.multiple_of(s * size, 8), size), :] = jnp.concatenate(picked, axis=0)
            return carry

        lax.fori_loop(0, blocks // SLOT_STEP, step, 0)

    def call(mine, other, rows, film, x):
        vmem = pl.BlockSpec(memory_space=pltpu.VMEM)
        return pl.pallas_call(
            kernel,
            in_specs=[vmem] * 5,
            out_shape=[
                jax.ShapeDtypeStruct((blocks * per, L), f32),
                jax.ShapeDtypeStruct((ITERS * tall, L), f32),
                jax.ShapeDtypeStruct((2 * tall, L), f32),
            ],
            name="surface_lookup",
        )(mine, other, rows, film, x)

    return call


def face_finish(nl, width, blocks, capacity):
    c = FACE_CHUNK
    steps = width // c
    tall = width // L
    part = c // L
    highs = blocks * capacity // L

    def kernel(live_ref, reply_ref, slot_ref, y_ref, coef_ref, source_ref, surface_ref, out_ref, found_ref, rows_ref, table):
        i = pl.program_id(0)
        gas = lax.axis_index("grp") == 0

        @pl.when(i == 0)
        def _():
            high, low = split(reply_ref[...].T)
            table[...] = jnp.concatenate([high, low], axis=1).astype(bf16)

        slot = slot_ref[...]
        hot = onehot(iota((highs, c), 0) == (slot >> 7))
        found = dot(table[...], jnp.concatenate([hot, hot], axis=0))
        low = iota((L, c), 0) == (slot & (L - 1))
        live = (iota((1, c), 1) + i * c) < live_ref[0]
        picked = jnp.where(live, jnp.sum(jnp.where(low, found, 0.0), axis=0, keepdims=True), 0.0)
        found_ref[...] = picked

        coef = coef_ref[...]
        spread = [jnp.broadcast_to(coef[:, n : n + 1], (nl, L)) for n in range(ITERS)]
        first = []
        for k in range(part):
            cut = slice(k * L, (k + 1) * L)
            lead = jnp.where(gas, picked[:, cut], source_ref[0, k : k + 1])
            total = y_ref[:, cut] + spread[0] * lead
            for n in range(1, ITERS):
                total = total + spread[n] * source_ref[n, k : k + 1]
            out_ref[:, cut] = total
            rows_ref[0:1, cut] = jnp.where(gas, picked[:, cut], surface_ref[0, k : k + 1])
            rows_ref[1:2, cut] = surface_ref[1, k : k + 1]

    def call(live_count, reply, slot, y, coef, source, surface):
        row = pl.BlockSpec((1, c), lambda i: (0, i))
        wide = pl.BlockSpec((nl, c), lambda i: (0, i))
        return pl.pallas_call(
            kernel,
            grid=(steps,),
            in_specs=[
                pl.BlockSpec(memory_space=pltpu.SMEM),
                pl.BlockSpec((highs, L), lambda i: (0, 0)),
                row,
                wide,
                pl.BlockSpec((nl, L), lambda i: (0, 0)),
                pl.BlockSpec((ITERS, part, L), lambda i: (0, i, 0)),
                pl.BlockSpec((2, part, L), lambda i: (0, i, 0)),
            ],
            out_specs=[wide, row, pl.BlockSpec((2, c), lambda i: (0, i))],
            out_shape=[
                jax.ShapeDtypeStruct((nl, width), f32),
                jax.ShapeDtypeStruct((1, width), f32),
                jax.ShapeDtypeStruct((2, width), f32),
            ],
            scratch_shapes=[pltpu.VMEM((L, 2 * highs), bf16)],
            name="face_finish",
        )(live_count, reply, slot, y, coef, source.reshape(ITERS, tall, L), surface.reshape(2, tall, L))

    return call


def local(columns, operators, normal_weights, face_patch, face_point, live_count, impinged, crystal_load, film):
    nl, width = columns.shape[1:]
    blocks = lax.axis_size("blk")
    capacity = 2 * width // blocks
    per = capacity // L
    gas = lax.axis_index("grp") == 0
    side, matrix = columns[0], operators[0]
    swap = [(i, blocks + i) for i in range(blocks)] + [(blocks + i, i) for i in range(blocks)]

    def across(x):
        return lax.ppermute(x, ("grp", "blk"), swap)

    def exchange(x):
        return lax.all_to_all(x.reshape(-1), "blk", split_axis=0, concat_axis=0, tiled=True).reshape(x.shape)

    faces = [x.reshape(1, width) for x in (face_patch, face_point, impinged, crystal_load)]
    message, slot = route(width, blocks, capacity)(live_count, *faces, side, normal_weights)
    arrived = exchange(message)
    y, rows, coef = matrices(nl, width)(matrix, normal_weights, side)
    rows = jnp.where(gas, across(rows), rows)

    mine = gather_sum(width, blocks, capacity)(arrived)
    film = film.reshape(width // L, L)
    replies, source, surface = surface_lookup(width, blocks, capacity)(mine, across(mine), rows, film, arrived)
    returned = exchange(replies)
    new_columns, found, surface = face_finish(nl, width, blocks, capacity)(live_count, returned, slot, y, coef, source, surface)
    bottom = lax.broadcasted_iota(i32, surface.shape, 0) == 1
    surface = jnp.where(gas & bottom, across(found), surface)
    return new_columns[None], surface[None]


def solution(mesh):
    return jax.shard_map(
        local,
        mesh=mesh,
        in_specs=(
            P("grp", None, "blk"),
            P("grp", None, None),
            P(),
            P("blk", None),
            P("blk"),
            P("blk"),
            P("blk"),
            P("blk"),
            P("blk"),
        ),
        out_specs=(P("grp", None, "blk"), P("grp", None, "blk")),
        check_vma=False,
    )
```

```python
import jax
import jax.numpy as jnp
from jax import lax
from jax.experimental import pallas as pl
from jax.experimental.pallas import tpu as pltpu
from jax.sharding import PartitionSpec as P

ITERS = 4
L = 128
HALO = ITERS
ROWS = 11
FACE_CHUNK = 2048
SLOT_STEP = 8

f32 = jnp.float32
bf16 = jnp.bfloat16
i32 = jnp.int32
HIGHEST = lax.Precision.HIGHEST
NT = (((1,), (1,)), ((), ()))
NN = (((1,), (0,)), ((), ()))


def iota(shape, dim):
    return lax.broadcasted_iota(i32, shape, dim)


def split(x):
    high = x.astype(bf16).astype(f32)
    return high, x - high


def dot(a, b, dims=NN, precision=None):
    return lax.dot_general(a, b, dims, precision=precision, preferred_element_type=f32)


def counter(count, n):
    return jnp.concatenate([iota((count, L), 0).astype(f32).astype(bf16)] * (n // L), axis=1)


def spread(x):
    return jnp.broadcast_to(x, (16, x.shape[1])).astype(bf16)


def halves(x):
    rows = jnp.broadcast_to(x, (16, x.shape[1]))
    high = rows.astype(bf16)
    return high, (rows - high.astype(f32)).astype(bf16)


def tiled(rows, count):
    return jnp.concatenate([rows] * (count // 16), axis=0)


def hits(x, count):
    return counter(count, x.shape[1]) == tiled(spread(x), count)


def onehot(mask):
    return jnp.where(mask, jnp.ones(mask.shape, bf16), jnp.zeros(mask.shape, bf16))


def masked(mask, rows):
    return jnp.where(mask, tiled(rows, mask.shape[0]), jnp.zeros(mask.shape, bf16))


def transposed(x):
    m, n = x.shape
    if n < L:
        x = jnp.concatenate([x, jnp.zeros((m, L - n), f32)], axis=1)
    if m < L:
        x = jnp.concatenate([x, jnp.zeros((L - m, L), f32)], axis=0)
    return x.T


def edge_of(patch, point, width):
    last = point >= width - 3
    return (
        jnp.where(last, patch + 1, jnp.where(point < 3, patch - 1, -1)),
        jnp.where(last, point - (width - 8), point),
    )


def route(width, blocks, capacity):
    c = FACE_CHUNK
    steps = width // c
    per = capacity // L
    highs = blocks * per
    sub = 256

    def kernel(
        live_ref,
        patch_ref,
        point_ref,
        impinged_ref,
        load_ref,
        side_ref,
        before_ref,
        after_ref,
        weight_ref,
        out_ref,
        slot_ref,
        carry,
        acc,
        spots,
        eacc,
        weight,
        first_face,
        first_side,
    ):
        i = pl.program_id(0)
        gas = lax.axis_index("grp") == 0
        patch, point, side = patch_ref[...], point_ref[...], side_ref[...]

        @pl.when(i == 0)
        def _():
            carry[...] = jnp.zeros_like(carry)
            acc[...] = jnp.zeros_like(acc)
            eacc[...] = jnp.zeros_like(eacc)
            nl = side.shape[0]
            weight[...] = transposed(weight_ref[...])[:nl]
            first_face[0:1, :] = patch[:, :L]
            first_face[1:2, :] = point[:, :L]
            first_side[...] = side[:, :L]

        named = iota((blocks, c), 0) == patch
        hot = onehot(hits(patch.astype(f32), blocks))
        wide = (sub, sub + L)
        upto = jnp.where((iota(wide, 0) <= iota(wide, 1)) | (iota(wide, 1) >= sub), 1.0, 0.0).astype(bf16)
        before = carry[...]
        ranks = []
        for j in range(c // sub):
            cut = slice(j * sub, (j + 1) * sub)
            count = dot(hot[:, cut], upto)
            total = count[:, :sub] + jnp.concatenate([before] * (sub // L), axis=1)
            ranks.append(jnp.sum(jnp.where(named[:, cut], total, 0.0), axis=0, keepdims=True))
            before = before + count[:, sub:]
        carry[...] = before
        rank = jnp.concatenate(ranks, axis=1).astype(i32) - 1
        slot = patch * capacity + rank
        slot_ref[...] = slot

        lane = iota((1, c), 1)
        live = (lane + i * c) < live_ref[0]
        row = side[0:1]
        ahead = jnp.where(lane == c - 1, jnp.where(i == steps - 1, 0.0, after_ref[0:1, 0:1]), pltpu.roll(row, c - 1, 1))
        behind = jnp.where(lane == 0, jnp.where(i == 0, 0.0, before_ref[0:1, L - 1 : L]), pltpu.roll(row, 1, 1))
        flux = jnp.sum(weight[:, 0:1] * side, axis=0, keepdims=True) + 0.25 * (behind + ahead - 2.0 * row)
        crystal = impinged_ref[...].astype(f32) * load_ref[...]
        value = jnp.where(live, jnp.where(gas, flux, crystal), 0.0)
        v_high, v_low = split(value)
        t_high, t_low = ((point >> 7).astype(f32), (point & (L - 1)).astype(f32))
        high = onehot(hits((slot >> 7).astype(f32), highs))
        low = hits((slot & (L - 1)).astype(f32), L)
        laid = jnp.concatenate([masked(low, x) for x in (*halves(value), spread(t_high), spread(t_low))], axis=0)
        placed = dot(laid, high, NT)
        for q in range(4):
            acc[pl.ds(q * L, L), :] += placed[q * L : (q + 1) * L]

        edge_patch, edge_point = edge_of(patch, point, width)
        edge_hot = onehot(hits(edge_patch.astype(f32), blocks))
        edge_low = iota((8, c), 0) == edge_point
        edges = jnp.concatenate([jnp.where(edge_low, x, 0.0) for x in (v_high, v_low)], axis=0).astype(bf16)
        eacc[...] += dot(edges, edge_hot, NT)

        @pl.when(i == steps - 1)
        def _():
            spots[pl.ds(0, highs), :] = (acc[:L] + acc[L : 2 * L]).T
            spots[pl.ds(highs, highs), :] = (acc[2 * L : 3 * L] * float(L) + acc[3 * L :]).T
            for r in range(per):
                for q in range(2):
                    out_ref[pl.ds(q * per + r, blocks, stride=ROWS), :] = spots[pl.ds(q * highs + r, blocks, stride=per), :]
            spot, to = iota((blocks, L), 1), iota((blocks, L), 0)
            info = transposed(eacc[0:8] + eacc[8:16])[:blocks]
            info = jnp.where((spot == 8) & gas, first_side[0:1, 0:1], info)
            info = jnp.where((spot == 9) & gas, row[:, c - 1 :], info)
            ends = (
                (10, first_face[0:1, 0:1], first_face[1:2, 0:1], live_ref[0] > 0),
                (11, patch[:, c - 1 :], point[:, c - 1 :], live_ref[0] >= width),
            )
            for at, name, target, alive in ends:
                info = jnp.where(spot == at, jnp.where((to == name) & alive, target.astype(f32), -1.0), info)
                name, target = edge_of(name, target, width)
                info = jnp.where(spot == at + 2, jnp.where((to == name) & alive, target.astype(f32), -1.0), info)
            out_ref[pl.ds(2 * per, blocks, stride=ROWS), :] = info
            block = lax.axis_index("blk")
            half = spot[:1] < L // 2
            left, right = transposed(first_side[...]), transposed(side[:, c - L :])
            for r in range(2):
                rows = []
                for ends, base in ((left, 0), (right, L - HALO)):
                    j = base + 2 * r
                    rows.append(jnp.where(half, ends[j : j + 1], pltpu.roll(ends[j + 1 : j + 2], L // 2, 1)))
                sent = jnp.where(to == block - 1, rows[0], jnp.where(to == block + 1, rows[1], 0.0))
                out_ref[pl.ds(2 * per + 1 + r, blocks, stride=ROWS), :] = sent

    def call(live_count, patch, point, impinged, load, side, weights):
        nl = side.shape[0]
        row = pl.BlockSpec((1, c), lambda i: (0, i))
        return pl.pallas_call(
            kernel,
            grid=(steps,),
            in_specs=[
                pl.BlockSpec(memory_space=pltpu.SMEM),
                row,
                row,
                row,
                row,
                pl.BlockSpec((nl, c), lambda i: (0, i)),
                pl.BlockSpec((8, L), lambda i: (0, jnp.maximum(i * (c // L) - 1, 0))),
                pl.BlockSpec((8, L), lambda i: (0, jnp.minimum((i + 1) * (c // L), width // L - 1))),
                pl.BlockSpec(weights.shape, lambda i: (0, 0)),
            ],
            out_specs=[pl.BlockSpec((blocks * ROWS, L), lambda i: (0, 0)), row],
            out_shape=[
                jax.ShapeDtypeStruct((blocks * ROWS, L), f32),
                jax.ShapeDtypeStruct((1, width), i32),
            ],
            scratch_shapes=[
                pltpu.VMEM((blocks, L), f32),
                pltpu.VMEM((4 * L, highs), f32),
                pltpu.VMEM((2 * highs, L), f32),
                pltpu.VMEM((16, blocks), f32),
                pltpu.VMEM((nl, L), f32),
                pltpu.VMEM((8, L), i32),
                pltpu.VMEM((nl, L), f32),
            ],
            name="route",
        )(live_count, patch, point, impinged, load, side, side, side, weights)

    return call


def matrices(nl, width):
    c = FACE_CHUNK
    steps = width // c
    out_rows = nl + 8
    tail = (ITERS + 1) * width // L

    def kernel(op_ref, weight_ref, side_ref, y_ref, rows_ref, coef_ref, lhs):
        i = pl.program_id(0)

        @pl.when(i == 0)
        def _():
            gas = lax.axis_index("grp") == 0
            coupling = transposed(weight_ref[...])[:nl, 1:2]
            one = op_ref[...]
            two = dot(one, one, precision=HIGHEST)
            three = dot(two, one, precision=HIGHEST)
            four = dot(two, two, precision=HIGHEST)
            main = jnp.where(gas, one, four)
            unit = jnp.where(iota((1, nl), 1) == 0, 1.0, 0.0)
            full = jnp.concatenate([main, unit, one[0:1], two[0:1], three[0:1], four[0:1], jnp.zeros((3, nl), f32)], axis=0)
            high, low = split(full)
            lhs[...] = jnp.concatenate([high, low, high, low], axis=1).astype(bf16)
            rows_ref[pl.ds(tail, 8), :] = jnp.concatenate([full[nl:], jnp.zeros((8, L - nl), f32)], axis=1)
            lead = [jnp.broadcast_to(m[0:1, 0:1], (1, L)) for m in (one, two, three, four)]
            rows_ref[pl.ds(tail + 8, 8), :] = jnp.concatenate(lead + [jnp.zeros((4, L), f32)], axis=0)
            lane = iota((nl, L), 1)
            coef = jnp.where(lane == 0, jnp.where(gas, coupling, four[:, 0:1]), 0.0)
            for k, m in ((1, three), (2, two), (3, one)):
                coef = jnp.where(lane == k, jnp.where(gas, 0.0, m[:, 0:1]), coef)
            coef_ref[...] = coef

        high, low = split(side_ref[...])
        high, low = high.astype(bf16), low.astype(bf16)
        out = dot(lhs[...], jnp.concatenate([high, high, low, low], axis=0))
        y_ref[...] = out[:nl]
        for n in range(ITERS + 1):
            part = [out[nl + n : nl + n + 1, k * L : (k + 1) * L] for k in range(c // L)]
            start = pl.multiple_of(n * (width // L) + i * (c // L), 8)
            rows_ref[pl.ds(start, c // L), :] = jnp.concatenate(part, axis=0)

    def call(op, weights, side):
        return pl.pallas_call(
            kernel,
            grid=(steps,),
            in_specs=[
                pl.BlockSpec((nl, nl), lambda i: (0, 0)),
                pl.BlockSpec(weights.shape, lambda i: (0, 0)),
                pl.BlockSpec((nl, c), lambda i: (0, i)),
            ],
            out_specs=[
                pl.BlockSpec((nl, c), lambda i: (0, i)),
                pl.BlockSpec((tail + 16, L), lambda i: (0, 0)),
                pl.BlockSpec((nl, L), lambda i: (0, 0)),
            ],
            out_shape=[
                jax.ShapeDtypeStruct((nl, width), f32),
                jax.ShapeDtypeStruct((tail + 16, L), f32),
                jax.ShapeDtypeStruct((nl, L), f32),
            ],
            scratch_shapes=[pltpu.VMEM((out_rows, 4 * nl), bf16)],
            name="matrices",
        )(op, weights, side)

    return call


def gather_sum(width, blocks, capacity):
    per = capacity // L
    tall = width // L

    def kernel(x_ref, out_ref, acc):
        def step(s, nothing):
            start = pl.multiple_of(s * SLOT_STEP * ROWS, 8)
            x = x_ref[pl.ds(start, SLOT_STEP * ROWS), :]
            t = x.astype(i32)
            t_high, t_low = (t >> 7).astype(f32), (t & (L - 1)).astype(f32)
            highs, lows = [], []
            for m in range(SLOT_STEP):
                for r in range(per):
                    a, b = m * ROWS + r, m * ROWS + per + r
                    highs.append(onehot(hits(t_high[b : b + 1], tall)))
                    low = hits(t_low[b : b + 1], L)
                    lows.append(jnp.concatenate([masked(low, part) for part in halves(x[a : a + 1])], axis=0))
            acc[...] += dot(jnp.concatenate(highs, axis=1), jnp.concatenate(lows, axis=1), NT)
            return nothing

        info = x_ref[pl.ds(2 * per, blocks, stride=ROWS), :]
        across = transposed(info)
        lane = iota((1, L), 1)
        left = lane < blocks

        def ends(a, b):
            return jnp.where(left, a, pltpu.roll(b, blocks, 1))

        value = 0.25 * ends(pltpu.roll(across[9:10], 1, 1), pltpu.roll(across[8:9], L - 1, 1))
        target = ends(across[10:11], across[11:12]).astype(i32)
        halo = ends(across[12:13], across[13:14]).astype(i32)
        v_high, v_low = split(value)
        low = hits((target & (L - 1)).astype(f32), L)
        high = onehot(hits((target >> 7).astype(f32), tall))
        acc[...] = dot(high, jnp.concatenate([masked(low, x) for x in halves(value)], axis=0), NT)
        at = onehot(hits(halo.astype(f32), L))
        pieces = jnp.concatenate([v_high, v_low, jnp.zeros((6, L), f32)], axis=0).astype(bf16)
        edge = jnp.sum(dot(pieces, at, NT), axis=0, keepdims=True)
        edge = edge + jnp.where(lane < 8, jnp.sum(info, axis=0, keepdims=True), 0.0)

        lax.fori_loop(0, blocks // SLOT_STEP, step, 0)
        out_ref[pl.ds(0, tall), :] = acc[:, :L] + acc[:, L:]
        block, source = lax.axis_index("blk"), iota((blocks, L), 0)
        rows = [edge]
        for near in (block - 1, block + 1):
            for r in range(2):
                columns = x_ref[pl.ds(2 * per + 1 + r, blocks, stride=ROWS), :]
                rows.append(jnp.sum(jnp.where(source == near, columns, 0.0), axis=0, keepdims=True))
        out_ref[pl.ds(tall, 8), :] = jnp.concatenate(rows + [jnp.zeros((3, L), f32)], axis=0)

    def call(x):
        return pl.pallas_call(
            kernel,
            out_shape=jax.ShapeDtypeStruct((tall + 8, L), f32),
            scratch_shapes=[pltpu.VMEM((tall, 2 * L), f32)],
            name="gather_sum",
        )(x)

    return call


def surface_lookup(width, blocks, capacity):
    per = capacity // L
    tall = width // L
    ext = tall + 16

    def kernel(mine_ref, other_ref, rows_mine, rows_other, film_ref, x_ref, out_ref, source_ref, surface_ref):
        gas = lax.axis_index("grp") == 0
        block = lax.axis_index("blk")
        lane, line = iota((ext, L), 1), iota((ext, L), 0)
        inside = (line >= 8) & (line < tall + 8)
        left = (line == 7) & (lane >= L - HALO)
        right = (line == tall + 8) & (lane < HALO)
        valid = inside | (left & (block > 0)) | (right & (block < blocks - 1))

        def extend(body, edge_left, edge_right):
            zeros = jnp.zeros((7, L), f32)
            full = jnp.concatenate([zeros, edge_left, body, edge_right, zeros], axis=0)
            return jnp.where(valid, full, 0.0)

        def lateral(x):
            ahead = pltpu.roll(x, L - 1, 1)
            ahead = jnp.where(lane == L - 1, pltpu.roll(ahead, ext - 1, 0), ahead)
            behind = pltpu.roll(x, 1, 1)
            behind = jnp.where(lane == 0, pltpu.roll(behind, 1, 0), behind)
            return behind + ahead - 2.0 * x

        mine, other = mine_ref[...], other_ref[...]
        heat, mass = jnp.where(gas, mine, other), jnp.where(gas, other, mine)
        q = heat - 0.5 * mass
        q_edge = q[tall : tall + 1]
        q = extend(q[:tall], pltpu.roll(q_edge, L - 8, 1), q_edge)
        tail = (ITERS + 1) * tall

        def rows(start, size):
            cut = pl.ds(start, size)
            return jnp.where(gas, rows_other[cut, :], rows_mine[cut, :])

        lead = rows(tail + 8, 8)
        near = jnp.where(gas, other[tall:], mine[tall:])
        half = lane[:1] < L // 2

        def columns(a):
            for x in (near[a : a + 1], near[a + 1 : a + 2]):
                yield jnp.where(half, x, 0.0)
                yield jnp.where(half, pltpu.roll(x, L // 2, 1), 0.0)

        gap = jnp.zeros((L - 2 * HALO, L), f32)
        halo = jnp.concatenate([*columns(3), gap, *columns(1)], axis=0)
        halo = dot(rows(tail, 8), halo, NT, precision=HIGHEST)

        def base(n):
            edge = halo[n : n + 1]
            return extend(rows(n * tall, tall), edge, edge)

        sources = []
        row = base(0)
        for n in range(1, ITERS + 1):
            sources.append(0.2 * (q + 0.5 * lateral(row)))
            row = base(n)
            for j, source in enumerate(sources):
                row = row + lead[n - 1 - j : n - j] * source
            row = jnp.where(valid, row, 0.0)
        for n in range(ITERS):
            source_ref[pl.ds(n * tall, tall), :] = sources[n][8 : tall + 8]
        wall_row = row[8 : tall + 8]
        film_new = jnp.maximum(film_ref[...] + 0.5 * (wall_row - 0.3) - 0.1 * mass[:tall], 0.0)
        surface_ref[pl.ds(0, tall), :] = wall_row
        surface_ref[pl.ds(tall, tall), :] = film_new

        high, low = split(jnp.where(gas, wall_row, film_new).T)
        table = jnp.concatenate([high, low], axis=1).astype(bf16)

        def step(s, carry):
            start = pl.multiple_of(s * SLOT_STEP * ROWS, 8)
            t = x_ref[pl.ds(start, SLOT_STEP * ROWS), :].astype(i32)
            t_high, t_low = (t >> 7).astype(f32), t & (L - 1)
            rows = [m * ROWS + per + r for m in range(SLOT_STEP) for r in range(per)]
            highs = jnp.concatenate([onehot(hits(t_high[b : b + 1], tall)) for b in rows], axis=1)
            found = dot(table, jnp.concatenate([highs, highs], axis=0))
            picked = []
            for k, b in enumerate(rows):
                low = iota((L, L), 0) == t_low[b : b + 1]
                picked.append(jnp.sum(jnp.where(low, found[:, k * L : (k + 1) * L], 0.0), axis=0, keepdims=True))
            size = SLOT_STEP * per
            out_ref[pl.ds(pl.multiple_of(s * size, 8), size), :] = jnp.concatenate(picked, axis=0)
            return carry

        lax.fori_loop(0, blocks // SLOT_STEP, step, 0)

    def call(*args):
        vmem = pl.BlockSpec(memory_space=pltpu.VMEM)
        return pl.pallas_call(
            kernel,
            in_specs=[vmem] * 6,
            out_shape=[
                jax.ShapeDtypeStruct((blocks * per, L), f32),
                jax.ShapeDtypeStruct((ITERS * tall, L), f32),
                jax.ShapeDtypeStruct((2 * tall, L), f32),
            ],
            name="surface_lookup",
        )(*args)

    return call


def add_sources(nl, width):
    c = FACE_CHUNK
    tall = width // L
    part = c // L

    def kernel(y_ref, coef_ref, source_ref, out_ref):
        gas = lax.axis_index("grp") == 0

        @pl.when(gas)
        def _():
            out_ref[...] = y_ref[...]

        @pl.when(jnp.logical_not(gas))
        def _():
            coef = coef_ref[...]
            spread = [jnp.broadcast_to(coef[:, n : n + 1], (nl, L)) for n in range(ITERS)]
            for k in range(part):
                cut = slice(k * L, (k + 1) * L)
                total = y_ref[:, cut]
                for n in range(ITERS):
                    total = total + spread[n] * source_ref[n, k : k + 1]
                out_ref[:, cut] = total

    def call(y, coef, source):
        wide = pl.BlockSpec((nl, c), lambda i: (0, i))
        return pl.pallas_call(
            kernel,
            grid=(width // c,),
            in_specs=[
                wide,
                pl.BlockSpec((nl, L), lambda i: (0, 0)),
                pl.BlockSpec((ITERS, part, L), lambda i: (0, i, 0)),
            ],
            out_specs=wide,
            out_shape=jax.ShapeDtypeStruct((nl, width), f32),
            name="add_sources",
        )(y, coef, source.reshape(ITERS, tall, L))

    return call


def face_finish(nl, width, blocks, capacity):
    c = FACE_CHUNK
    steps = width // c
    tall = width // L
    part = c // L
    highs = blocks * capacity // L

    def kernel(live_ref, reply_ref, slot_ref, y_ref, coef_ref, surface_ref, out_ref, found_ref, rows_ref, table):
        i = pl.program_id(0)
        gas = lax.axis_index("grp") == 0

        @pl.when(i == 0)
        def _():
            high, low = split(reply_ref[...].T)
            table[...] = jnp.concatenate([high, low], axis=1).astype(bf16)

        slot = slot_ref[...]
        hot = onehot(hits((slot >> 7).astype(f32), highs))
        found = dot(table[...], jnp.concatenate([hot, hot], axis=0))
        low = iota((L, c), 0) == (slot & (L - 1))
        live = (iota((1, c), 1) + i * c) < live_ref[0]
        picked = jnp.where(live, jnp.sum(jnp.where(low, found, 0.0), axis=0, keepdims=True), 0.0)
        found_ref[...] = picked

        coupling = jnp.broadcast_to(jnp.where(gas, coef_ref[:, 0:1], 0.0), (nl, L))
        for k in range(part):
            cut = slice(k * L, (k + 1) * L)
            out_ref[:, cut] = y_ref[:, cut] + coupling * picked[:, cut]
            rows_ref[0:1, cut] = jnp.where(gas, picked[:, cut], surface_ref[0, k : k + 1])
            rows_ref[1:2, cut] = surface_ref[1, k : k + 1]

    def call(live_count, reply, slot, y, coef, surface):
        row = pl.BlockSpec((1, c), lambda i: (0, i))
        wide = pl.BlockSpec((nl, c), lambda i: (0, i))
        return pl.pallas_call(
            kernel,
            grid=(steps,),
            in_specs=[
                pl.BlockSpec(memory_space=pltpu.SMEM),
                pl.BlockSpec((highs, L), lambda i: (0, 0)),
                row,
                wide,
                pl.BlockSpec((nl, L), lambda i: (0, 0)),
                pl.BlockSpec((2, part, L), lambda i: (0, i, 0)),
            ],
            out_specs=[wide, row, pl.BlockSpec((2, c), lambda i: (0, i))],
            out_shape=[
                jax.ShapeDtypeStruct((nl, width), f32),
                jax.ShapeDtypeStruct((1, width), f32),
                jax.ShapeDtypeStruct((2, width), f32),
            ],
            scratch_shapes=[pltpu.VMEM((L, 2 * highs), bf16)],
            name="face_finish",
        )(live_count, reply, slot, y, coef, surface.reshape(2, tall, L))

    return call


def local(columns, operators, normal_weights, face_patch, face_point, live_count, impinged, crystal_load, film):
    nl, width = columns.shape[1:]
    blocks = lax.axis_size("blk")
    capacity = 2 * width // blocks
    per = capacity // L
    gas = lax.axis_index("grp") == 0
    side, matrix = columns[0], operators[0]
    swap = [(i, blocks + i) for i in range(blocks)] + [(blocks + i, i) for i in range(blocks)]

    def across(x):
        return lax.ppermute(x, ("grp", "blk"), swap)

    def exchange(x):
        return lax.all_to_all(x.reshape(-1), "blk", split_axis=0, concat_axis=0, tiled=True).reshape(x.shape)

    faces = [x.reshape(1, width) for x in (face_patch, face_point, impinged, crystal_load)]
    message, slot = route(width, blocks, capacity)(live_count, *faces, side, normal_weights)
    arrived = exchange(message)
    y, rows, coef = matrices(nl, width)(matrix, normal_weights, side)
    rows_other = across(rows)

    mine = gather_sum(width, blocks, capacity)(arrived)
    film = film.reshape(width // L, L)
    replies, source, surface = surface_lookup(width, blocks, capacity)(mine, across(mine), rows, rows_other, film, arrived)
    returned = exchange(replies)
    y = add_sources(nl, width)(y, coef, source)
    new_columns, found, surface = face_finish(nl, width, blocks, capacity)(live_count, returned, slot, y, coef, surface)
    bottom = lax.broadcasted_iota(i32, surface.shape, 0) == 1
    surface = jnp.where(gas & bottom, across(found), surface)
    return new_columns[None], surface[None]


def solution(mesh):
    return jax.shard_map(
        local,
        mesh=mesh,
        in_specs=(
            P("grp", None, "blk"),
            P("grp", None, None),
            P(),
            P("blk", None),
            P("blk"),
            P("blk"),
            P("blk"),
            P("blk"),
            P("blk"),
        ),
        out_specs=(P("grp", None, "blk"), P("grp", None, "blk")),
        check_vma=False,
    )
```

```python
import jax
import jax.numpy as jnp
from jax import lax
from jax.experimental import pallas as pl
from jax.experimental.pallas import tpu as pltpu
from jax.sharding import PartitionSpec as P

ITERS = 4
L = 128
HALO = ITERS
PARAMS = pltpu.CompilerParams(vmem_limit_bytes=24 << 20)
MIDDLE = pltpu.CompilerParams(vmem_limit_bytes=52 << 20)
LARGE = pltpu.CompilerParams(vmem_limit_bytes=60 << 20)
ROWS = 11
FACE_CHUNK = 2048
PIECE = 256
SLOT_STEP = 8

f32 = jnp.float32
bf16 = jnp.bfloat16
i32 = jnp.int32
HIGHEST = lax.Precision.HIGHEST
NT = (((1,), (1,)), ((), ()))
NN = (((1,), (0,)), ((), ()))


def iota(shape, dim):
    return lax.broadcasted_iota(i32, shape, dim)


def split(x):
    high = x.astype(bf16).astype(f32)
    return high, x - high


def dot(a, b, dims=NN, precision=None):
    return lax.dot_general(a, b, dims, precision=precision, preferred_element_type=f32)


def counter(count, n):
    return jnp.concatenate([iota((count, L), 0).astype(f32).astype(bf16)] * (n // L), axis=1)


def spread(x):
    return jnp.broadcast_to(x, (16, x.shape[1])).astype(bf16)


def halves(x):
    rows = jnp.broadcast_to(x, (16, x.shape[1]))
    high = rows.astype(bf16)
    return high, (rows - high.astype(f32)).astype(bf16)


def tiled(rows, count):
    return jnp.concatenate([rows] * (count // 16), axis=0)


def hits(x, count):
    return counter(count, x.shape[1]) == tiled(spread(x), count)


def onehot(mask):
    return jnp.where(mask, jnp.ones(mask.shape, bf16), jnp.zeros(mask.shape, bf16))


def masked(mask, rows):
    return jnp.where(mask, tiled(rows, mask.shape[0]), jnp.zeros(mask.shape, bf16))


def transposed(x):
    m, n = x.shape
    if n < L:
        x = jnp.concatenate([x, jnp.zeros((m, L - n), f32)], axis=1)
    if m < L:
        x = jnp.concatenate([x, jnp.zeros((L - m, L), f32)], axis=0)
    return x.T


def edge_of(patch, point, width):
    last = point >= width - 3
    return (
        jnp.where(last, patch + 1, jnp.where(point < 3, patch - 1, -1)),
        jnp.where(last, point - (width - 8), point),
    )


def route(width, blocks, capacity):
    c = FACE_CHUNK
    steps = width // c
    per = capacity // L
    highs = blocks * per
    sub = 256

    def kernel(
        live_ref,
        patch_ref,
        point_ref,
        impinged_ref,
        load_ref,
        side_ref,
        before_ref,
        after_ref,
        weight_ref,
        out_ref,
        slot_ref,
        carry,
        acc,
        spots,
        eacc,
        weight,
        first_face,
        first_side,
    ):
        i = pl.program_id(0)
        gas = lax.axis_index("grp") == 0
        patch, point, side = patch_ref[...], point_ref[...], side_ref[...]

        @pl.when(i == 0)
        def _():
            carry[...] = jnp.zeros_like(carry)
            acc[...] = jnp.zeros_like(acc)
            eacc[...] = jnp.zeros_like(eacc)
            nl = side.shape[0]
            weight[...] = transposed(weight_ref[...])[:nl]
            first_face[0:1, :] = patch[:, :L]
            first_face[1:2, :] = point[:, :L]
            first_side[...] = side[:, :L]

        named = iota((blocks, c), 0) == patch
        hot = onehot(hits(patch.astype(f32), blocks))
        wide = (sub, sub + L)
        upto = jnp.where((iota(wide, 0) <= iota(wide, 1)) | (iota(wide, 1) >= sub), 1.0, 0.0).astype(bf16)
        cuts = [slice(j * sub, (j + 1) * sub) for j in range(c // sub)]
        counts = dot(jnp.concatenate([hot[:, cut] for cut in cuts], axis=0), upto)
        before = carry[...]
        ranks = []
        for j, cut in enumerate(cuts):
            count = counts[j * blocks : (j + 1) * blocks]
            total = count[:, :sub] + jnp.concatenate([before] * (sub // L), axis=1)
            ranks.append(jnp.sum(jnp.where(named[:, cut], total, 0.0), axis=0, keepdims=True))
            before = before + count[:, sub:]
        carry[...] = before
        rank = jnp.concatenate(ranks, axis=1).astype(i32) - 1
        slot = patch * capacity + rank
        slot_ref[...] = slot

        lane = iota((1, c), 1)
        live = (lane + i * c) < live_ref[0]
        row = side[0:1]
        ahead = jnp.where(lane == c - 1, jnp.where(i == steps - 1, 0.0, after_ref[0:1, 0:1]), pltpu.roll(row, c - 1, 1))
        behind = jnp.where(lane == 0, jnp.where(i == 0, 0.0, before_ref[0:1, L - 1 : L]), pltpu.roll(row, 1, 1))
        flux = jnp.sum(weight[:, 0:1] * side, axis=0, keepdims=True) + 0.25 * (behind + ahead - 2.0 * row)
        crystal = impinged_ref[...].astype(f32) * load_ref[...]
        value = jnp.where(live, jnp.where(gas, flux, crystal), 0.0)
        v_high, v_low = split(value)
        t_high, t_low = ((point >> 7).astype(f32), (point & (L - 1)).astype(f32))
        high = onehot(hits((slot >> 7).astype(f32), highs))
        low = hits((slot & (L - 1)).astype(f32), L)
        laid = jnp.concatenate([masked(low, x) for x in (*halves(value), spread(t_high), spread(t_low))], axis=0)
        placed = dot(laid, high, NT)
        for q in range(4):
            acc[pl.ds(q * L, L), :] += placed[q * L : (q + 1) * L]

        edge_patch, edge_point = edge_of(patch, point, width)
        edge_hot = onehot(hits(edge_patch.astype(f32), blocks))
        edge_low = iota((8, c), 0) == edge_point
        edges = jnp.concatenate([jnp.where(edge_low, x, 0.0) for x in (v_high, v_low)], axis=0).astype(bf16)
        eacc[...] += dot(edges, edge_hot, NT)

        @pl.when(i == steps - 1)
        def _():
            spots[pl.ds(0, highs), :] = (acc[:L] + acc[L : 2 * L]).T
            spots[pl.ds(highs, highs), :] = (acc[2 * L : 3 * L] * float(L) + acc[3 * L :]).T
            for r in range(per):
                for q in range(2):
                    out_ref[pl.ds(q * per + r, blocks, stride=ROWS), :] = spots[pl.ds(q * highs + r, blocks, stride=per), :]
            spot, to = iota((blocks, L), 1), iota((blocks, L), 0)
            info = transposed(eacc[0:8] + eacc[8:16])[:blocks]
            info = jnp.where((spot == 8) & gas, first_side[0:1, 0:1], info)
            info = jnp.where((spot == 9) & gas, row[:, c - 1 :], info)
            ends = (
                (10, first_face[0:1, 0:1], first_face[1:2, 0:1], live_ref[0] > 0),
                (11, patch[:, c - 1 :], point[:, c - 1 :], live_ref[0] >= width),
            )
            for at, name, target, alive in ends:
                info = jnp.where(spot == at, jnp.where((to == name) & alive, target.astype(f32), -1.0), info)
                name, target = edge_of(name, target, width)
                info = jnp.where(spot == at + 2, jnp.where((to == name) & alive, target.astype(f32), -1.0), info)
            out_ref[pl.ds(2 * per, blocks, stride=ROWS), :] = info
            block = lax.axis_index("blk")
            half = spot[:1] < L // 2
            left, right = transposed(first_side[...]), transposed(side[:, c - L :])
            for r in range(2):
                rows = []
                for ends, base in ((left, 0), (right, L - HALO)):
                    j = base + 2 * r
                    rows.append(jnp.where(half, ends[j : j + 1], pltpu.roll(ends[j + 1 : j + 2], L // 2, 1)))
                sent = jnp.where(to == block - 1, rows[0], jnp.where(to == block + 1, rows[1], 0.0))
                out_ref[pl.ds(2 * per + 1 + r, blocks, stride=ROWS), :] = sent

    def call(live_count, patch, point, impinged, load, side, weights):
        nl = side.shape[0]
        row = pl.BlockSpec((1, c), lambda i: (0, i))
        return pl.pallas_call(
            kernel,
            grid=(steps,),
            in_specs=[
                pl.BlockSpec(memory_space=pltpu.SMEM),
                row,
                row,
                row,
                row,
                pl.BlockSpec((nl, c), lambda i: (0, i)),
                pl.BlockSpec((8, L), lambda i: (0, jnp.maximum(i * (c // L) - 1, 0))),
                pl.BlockSpec((8, L), lambda i: (0, jnp.minimum((i + 1) * (c // L), width // L - 1))),
                pl.BlockSpec(weights.shape, lambda i: (0, 0)),
            ],
            out_specs=[pl.BlockSpec((blocks * ROWS, L), lambda i: (0, 0)), row],
            out_shape=[
                jax.ShapeDtypeStruct((blocks * ROWS, L), f32),
                jax.ShapeDtypeStruct((1, width), i32),
            ],
            scratch_shapes=[
                pltpu.VMEM((blocks, L), f32),
                pltpu.VMEM((4 * L, highs), f32),
                pltpu.VMEM((2 * highs, L), f32),
                pltpu.VMEM((16, blocks), f32),
                pltpu.VMEM((nl, L), f32),
                pltpu.VMEM((8, L), i32),
                pltpu.VMEM((nl, L), f32),
            ],
            compiler_params=LARGE,
            name="route",
        )(live_count, patch, point, impinged, load, side, side, side, weights)

    return call


def matrices(nl, width):
    c = FACE_CHUNK
    steps = width // c
    out_rows = nl + 8
    tail = (ITERS + 1) * width // L

    def kernel(op_ref, weight_ref, side_ref, y_ref, rows_ref, coef_ref, lhs):
        i = pl.program_id(0)

        @pl.when(i == 0)
        def _():
            gas = lax.axis_index("grp") == 0
            coupling = transposed(weight_ref[...])[:nl, 1:2]
            one = op_ref[...]
            two = dot(one, one, precision=HIGHEST)
            three = dot(two, one, precision=HIGHEST)
            four = dot(two, two, precision=HIGHEST)
            main = jnp.where(gas, one, four)
            unit = jnp.where(iota((1, nl), 1) == 0, 1.0, 0.0)
            full = jnp.concatenate([main, unit, one[0:1], two[0:1], three[0:1], four[0:1], jnp.zeros((3, nl), f32)], axis=0)
            high, low = split(full)
            lhs[...] = jnp.concatenate([high, low, high, low], axis=1).astype(bf16)
            rows_ref[pl.ds(tail, 8), :] = jnp.concatenate([full[nl:], jnp.zeros((8, L - nl), f32)], axis=1)
            lead = [jnp.broadcast_to(m[0:1, 0:1], (1, L)) for m in (one, two, three, four)]
            rows_ref[pl.ds(tail + 8, 8), :] = jnp.concatenate(lead + [jnp.zeros((4, L), f32)], axis=0)
            lane = iota((nl, L), 1)
            coef = jnp.where(lane == 0, jnp.where(gas, coupling, four[:, 0:1]), 0.0)
            for k, m in ((1, three), (2, two), (3, one)):
                coef = jnp.where(lane == k, jnp.where(gas, 0.0, m[:, 0:1]), coef)
            coef_ref[...] = coef

        high, low = split(side_ref[...])
        high, low = high.astype(bf16), low.astype(bf16)
        out = dot(lhs[...], jnp.concatenate([high, high, low, low], axis=0))
        y_ref[...] = out[:nl]
        for n in range(ITERS + 1):
            part = [out[nl + n : nl + n + 1, k * L : (k + 1) * L] for k in range(c // L)]
            start = pl.multiple_of(n * (width // L) + i * (c // L), 8)
            rows_ref[pl.ds(start, c // L), :] = jnp.concatenate(part, axis=0)

    def call(op, weights, side):
        return pl.pallas_call(
            kernel,
            grid=(steps,),
            in_specs=[
                pl.BlockSpec((nl, nl), lambda i: (0, 0)),
                pl.BlockSpec(weights.shape, lambda i: (0, 0)),
                pl.BlockSpec((nl, c), lambda i: (0, i)),
            ],
            out_specs=[
                pl.BlockSpec((nl, c), lambda i: (0, i)),
                pl.BlockSpec((tail + 16, L), lambda i: (0, 0)),
                pl.BlockSpec((nl, L), lambda i: (0, 0)),
            ],
            out_shape=[
                jax.ShapeDtypeStruct((nl, width), f32),
                jax.ShapeDtypeStruct((tail + 16, L), f32),
                jax.ShapeDtypeStruct((nl, L), f32),
            ],
            scratch_shapes=[pltpu.VMEM((out_rows, 4 * nl), bf16)],
            compiler_params=MIDDLE,
            name="matrices",
        )(op, weights, side)

    return call


def gather_sum(width, blocks, capacity):
    per = capacity // L
    tall = width // L

    def kernel(x_ref, out_ref, acc):
        def step(s, nothing):
            start = pl.multiple_of(s * SLOT_STEP * ROWS, 8)
            x = x_ref[pl.ds(start, SLOT_STEP * ROWS), :]
            t = x.astype(i32)
            t_high, t_low = (t >> 7).astype(f32), (t & (L - 1)).astype(f32)
            highs, lows = [], []
            for m in range(SLOT_STEP):
                for r in range(per):
                    a, b = m * ROWS + r, m * ROWS + per + r
                    highs.append(onehot(hits(t_high[b : b + 1], tall)))
                    low = hits(t_low[b : b + 1], L)
                    lows.append(jnp.concatenate([masked(low, part) for part in halves(x[a : a + 1])], axis=0))
            placed = dot(jnp.concatenate(lows, axis=1), jnp.concatenate(highs, axis=1), NT)
            for q in range(2):
                acc[pl.ds(q * L, L), :] += placed[q * L : (q + 1) * L]
            return nothing

        info = x_ref[pl.ds(2 * per, blocks, stride=ROWS), :]
        across = transposed(info)
        lane = iota((1, L), 1)
        left = lane < blocks

        def ends(a, b):
            return jnp.where(left, a, pltpu.roll(b, blocks, 1))

        value = 0.25 * ends(pltpu.roll(across[9:10], 1, 1), pltpu.roll(across[8:9], L - 1, 1))
        target = ends(across[10:11], across[11:12]).astype(i32)
        halo = ends(across[12:13], across[13:14]).astype(i32)
        v_high, v_low = split(value)
        low = hits((target & (L - 1)).astype(f32), L)
        high = onehot(hits((target >> 7).astype(f32), tall))
        acc[...] = dot(jnp.concatenate([masked(low, x) for x in halves(value)], axis=0), high, NT)
        at = onehot(hits(halo.astype(f32), L))
        pieces = jnp.concatenate([v_high, v_low, jnp.zeros((6, L), f32)], axis=0).astype(bf16)
        edge = jnp.sum(dot(pieces, at, NT), axis=0, keepdims=True)
        edge = edge + jnp.where(lane < 8, jnp.sum(info, axis=0, keepdims=True), 0.0)

        lax.fori_loop(0, blocks // SLOT_STEP, step, 0)
        out_ref[pl.ds(0, tall), :] = (acc[:L] + acc[L:]).T
        block, source = lax.axis_index("blk"), iota((blocks, L), 0)
        rows = [edge]
        for near in (block - 1, block + 1):
            for r in range(2):
                columns = x_ref[pl.ds(2 * per + 1 + r, blocks, stride=ROWS), :]
                rows.append(jnp.sum(jnp.where(source == near, columns, 0.0), axis=0, keepdims=True))
        out_ref[pl.ds(tall, 8), :] = jnp.concatenate(rows + [jnp.zeros((3, L), f32)], axis=0)

    def call(x):
        return pl.pallas_call(
            kernel,
            out_shape=jax.ShapeDtypeStruct((tall + 8, L), f32),
            scratch_shapes=[pltpu.VMEM((2 * L, tall), f32)],
            compiler_params=PARAMS,
            name="gather_sum",
        )(x)

    return call


def surface_lookup(width, blocks, capacity):
    per = capacity // L
    tall = width // L
    ext = tall + 16

    def kernel(mine_ref, other_ref, rows_mine, rows_other, film_ref, x_ref, out_ref, source_ref, surface_ref):
        gas = lax.axis_index("grp") == 0
        block = lax.axis_index("blk")
        lane, line = iota((ext, L), 1), iota((ext, L), 0)
        inside = (line >= 8) & (line < tall + 8)
        left = (line == 7) & (lane >= L - HALO)
        right = (line == tall + 8) & (lane < HALO)
        valid = inside | (left & (block > 0)) | (right & (block < blocks - 1))

        def extend(body, edge_left, edge_right):
            zeros = jnp.zeros((7, L), f32)
            full = jnp.concatenate([zeros, edge_left, body, edge_right, zeros], axis=0)
            return jnp.where(valid, full, 0.0)

        def lateral(x):
            ahead = pltpu.roll(x, L - 1, 1)
            ahead = jnp.where(lane == L - 1, pltpu.roll(ahead, ext - 1, 0), ahead)
            behind = pltpu.roll(x, 1, 1)
            behind = jnp.where(lane == 0, pltpu.roll(behind, 1, 0), behind)
            return behind + ahead - 2.0 * x

        mine, other = mine_ref[...], other_ref[...]
        heat, mass = jnp.where(gas, mine, other), jnp.where(gas, other, mine)
        q = heat - 0.5 * mass
        q_edge = q[tall : tall + 1]
        q = extend(q[:tall], pltpu.roll(q_edge, L - 8, 1), q_edge)
        tail = (ITERS + 1) * tall

        def rows(start, size):
            cut = pl.ds(start, size)
            return jnp.where(gas, rows_other[cut, :], rows_mine[cut, :])

        lead = rows(tail + 8, 8)
        near = jnp.where(gas, other[tall:], mine[tall:])
        half = lane[:1] < L // 2

        def columns(a):
            for x in (near[a : a + 1], near[a + 1 : a + 2]):
                yield jnp.where(half, x, 0.0)
                yield jnp.where(half, pltpu.roll(x, L // 2, 1), 0.0)

        gap = jnp.zeros((L - 2 * HALO, L), f32)
        halo = jnp.concatenate([*columns(3), gap, *columns(1)], axis=0)
        halo = dot(rows(tail, 8), halo, NT, precision=HIGHEST)

        def base(n):
            edge = halo[n : n + 1]
            return extend(rows(n * tall, tall), edge, edge)

        sources = []
        row = base(0)
        for n in range(1, ITERS + 1):
            sources.append(0.2 * (q + 0.5 * lateral(row)))
            row = base(n)
            for j, source in enumerate(sources):
                row = row + lead[n - 1 - j : n - j] * source
            row = jnp.where(valid, row, 0.0)
        for n in range(ITERS):
            source_ref[pl.ds(n * tall, tall), :] = sources[n][8 : tall + 8]
        wall_row = row[8 : tall + 8]
        film_new = jnp.maximum(film_ref[...] + 0.5 * (wall_row - 0.3) - 0.1 * mass[:tall], 0.0)
        surface_ref[pl.ds(0, tall), :] = wall_row
        surface_ref[pl.ds(tall, tall), :] = film_new

        high, low = split(jnp.where(gas, wall_row, film_new).T)
        table = jnp.concatenate([high, low], axis=1).astype(bf16)

        def step(s, carry):
            start = pl.multiple_of(s * SLOT_STEP * ROWS, 8)
            t = x_ref[pl.ds(start, SLOT_STEP * ROWS), :].astype(i32)
            t_high, t_low = (t >> 7).astype(f32), t & (L - 1)
            rows = [m * ROWS + per + r for m in range(SLOT_STEP) for r in range(per)]
            picked = []
            for g in range(0, len(rows), PIECE // L):
                group = rows[g : g + PIECE // L]
                highs = jnp.concatenate([onehot(hits(t_high[b : b + 1], tall)) for b in group], axis=1)
                found = dot(table, jnp.concatenate([highs, highs], axis=0))
                for k, b in enumerate(group):
                    low = iota((L, L), 0) == t_low[b : b + 1]
                    picked.append(jnp.sum(jnp.where(low, found[:, k * L : (k + 1) * L], 0.0), axis=0, keepdims=True))
            size = SLOT_STEP * per
            out_ref[pl.ds(pl.multiple_of(s * size, 8), size), :] = jnp.concatenate(picked, axis=0)
            return carry

        lax.fori_loop(0, blocks // SLOT_STEP, step, 0)

    def call(*args):
        vmem = pl.BlockSpec(memory_space=pltpu.VMEM)
        return pl.pallas_call(
            kernel,
            in_specs=[vmem] * 6,
            out_shape=[
                jax.ShapeDtypeStruct((blocks * per, L), f32),
                jax.ShapeDtypeStruct((ITERS * tall, L), f32),
                jax.ShapeDtypeStruct((2 * tall, L), f32),
            ],
            compiler_params=PARAMS,
            name="surface_lookup",
        )(*args)

    return call


def add_sources(nl, width):
    c = FACE_CHUNK
    tall = width // L
    part = c // L

    def kernel(y_ref, coef_ref, source_ref, out_ref):
        gas = lax.axis_index("grp") == 0

        @pl.when(gas)
        def _():
            out_ref[...] = y_ref[...]

        @pl.when(jnp.logical_not(gas))
        def _():
            coef = coef_ref[...]
            spread = [jnp.broadcast_to(coef[:, n : n + 1], (nl, L)) for n in range(ITERS)]
            for k in range(part):
                cut = slice(k * L, (k + 1) * L)
                total = y_ref[:, cut]
                for n in range(ITERS):
                    total = total + spread[n] * source_ref[n, k : k + 1]
                out_ref[:, cut] = total

    def call(y, coef, source):
        wide = pl.BlockSpec((nl, c), lambda i: (0, i))
        return pl.pallas_call(
            kernel,
            grid=(width // c,),
            in_specs=[
                wide,
                pl.BlockSpec((nl, L), lambda i: (0, 0)),
                pl.BlockSpec((ITERS, part, L), lambda i: (0, i, 0)),
            ],
            out_specs=wide,
            out_shape=jax.ShapeDtypeStruct((nl, width), f32),
            compiler_params=MIDDLE,
            name="add_sources",
        )(y, coef, source.reshape(ITERS, tall, L))

    return call


def face_finish(nl, width, blocks, capacity):
    c = FACE_CHUNK
    steps = width // c
    tall = width // L
    part = c // L
    highs = blocks * capacity // L

    def kernel(live_ref, reply_ref, slot_ref, y_ref, coef_ref, surface_ref, out_ref, found_ref, rows_ref, table):
        i = pl.program_id(0)
        gas = lax.axis_index("grp") == 0

        @pl.when(i == 0)
        def _():
            high, low = split(reply_ref[...].T)
            table[...] = jnp.concatenate([high, low], axis=0).astype(bf16)

        coupling = jnp.broadcast_to(jnp.where(gas, coef_ref[:, 0:1], 0.0), (nl, L))
        for j in range(c // PIECE):
            piece = slice(j * PIECE, (j + 1) * PIECE)
            slot = slot_ref[:, piece]
            hot = onehot(hits((slot >> 7).astype(f32), highs))
            found = dot(table[...], hot)
            found = found[:L] + found[L:]
            low = iota((L, PIECE), 0) == (slot & (L - 1))
            live = (iota((1, PIECE), 1) + (i * c + j * PIECE)) < live_ref[0]
            picked = jnp.where(live, jnp.sum(jnp.where(low, found, 0.0), axis=0, keepdims=True), 0.0)
            found_ref[:, piece] = picked
            for k in range(PIECE // L):
                m = j * (PIECE // L) + k
                cut = slice(m * L, (m + 1) * L)
                one = picked[:, k * L : (k + 1) * L]
                out_ref[:, cut] = y_ref[:, cut] + coupling * one
                rows_ref[0:1, cut] = jnp.where(gas, one, surface_ref[0, m : m + 1])
                rows_ref[1:2, cut] = surface_ref[1, m : m + 1]

    def call(live_count, reply, slot, y, coef, surface):
        row = pl.BlockSpec((1, c), lambda i: (0, i))
        wide = pl.BlockSpec((nl, c), lambda i: (0, i))
        return pl.pallas_call(
            kernel,
            grid=(steps,),
            in_specs=[
                pl.BlockSpec(memory_space=pltpu.SMEM),
                pl.BlockSpec((highs, L), lambda i: (0, 0)),
                row,
                wide,
                pl.BlockSpec((nl, L), lambda i: (0, 0)),
                pl.BlockSpec((2, part, L), lambda i: (0, i, 0)),
            ],
            out_specs=[wide, row, pl.BlockSpec((2, c), lambda i: (0, i))],
            out_shape=[
                jax.ShapeDtypeStruct((nl, width), f32),
                jax.ShapeDtypeStruct((1, width), f32),
                jax.ShapeDtypeStruct((2, width), f32),
            ],
            scratch_shapes=[pltpu.VMEM((2 * L, highs), bf16)],
            compiler_params=MIDDLE,
            name="face_finish",
        )(live_count, reply, slot, y, coef, surface.reshape(2, tall, L))

    return call


def local(columns, operators, normal_weights, face_patch, face_point, live_count, impinged, crystal_load, film):
    nl, width = columns.shape[1:]
    blocks = lax.axis_size("blk")
    capacity = 2 * width // blocks
    per = capacity // L
    gas = lax.axis_index("grp") == 0
    side, matrix = columns[0], operators[0]
    swap = [(i, blocks + i) for i in range(blocks)] + [(blocks + i, i) for i in range(blocks)]

    def across(x):
        return lax.ppermute(x, ("grp", "blk"), swap)

    def exchange(x):
        return lax.all_to_all(x.reshape(-1), "blk", split_axis=0, concat_axis=0, tiled=True).reshape(x.shape)

    faces = [x.reshape(1, width) for x in (face_patch, face_point, impinged, crystal_load)]
    message, slot = route(width, blocks, capacity)(live_count, *faces, side, normal_weights)
    arrived = exchange(message)
    y, rows, coef = matrices(nl, width)(matrix, normal_weights, side)
    rows_other = across(rows)

    mine = gather_sum(width, blocks, capacity)(arrived)
    film = film.reshape(width // L, L)
    replies, source, surface = surface_lookup(width, blocks, capacity)(mine, across(mine), rows, rows_other, film, arrived)
    returned = exchange(replies)
    y = add_sources(nl, width)(y, coef, source)
    new_columns, found, surface = face_finish(nl, width, blocks, capacity)(live_count, returned, slot, y, coef, surface)
    bottom = lax.broadcasted_iota(i32, surface.shape, 0) == 1
    surface = jnp.where(gas & bottom, across(found), surface)
    return new_columns[None], surface[None]


def solution(mesh):
    return jax.shard_map(
        local,
        mesh=mesh,
        in_specs=(
            P("grp", None, "blk"),
            P("grp", None, None),
            P(),
            P("blk", None),
            P("blk"),
            P("blk"),
            P("blk"),
            P("blk"),
            P("blk"),
        ),
        out_specs=(P("grp", None, "blk"), P("grp", None, "blk")),
        check_vma=False,
    )
```

```python
import jax
import jax.numpy as jnp
from jax import lax
from jax.experimental import pallas as pl
from jax.experimental.pallas import tpu as pltpu
from jax.sharding import PartitionSpec as P

ITERS = 4
L = 128
HALO = ITERS
PARAMS = pltpu.CompilerParams(vmem_limit_bytes=24 << 20)
MIDDLE = pltpu.CompilerParams(vmem_limit_bytes=52 << 20)
LARGE = pltpu.CompilerParams(vmem_limit_bytes=60 << 20)
ROWS = 9
FACE_CHUNK = 2048
PIECE = 256
SLOT_STEP = 8

f32 = jnp.float32
bf16 = jnp.bfloat16
i32 = jnp.int32
HIGHEST = lax.Precision.HIGHEST
NT = (((1,), (1,)), ((), ()))
NN = (((1,), (0,)), ((), ()))


def iota(shape, dim):
    return lax.broadcasted_iota(i32, shape, dim)


def split(x):
    high = x.astype(bf16).astype(f32)
    return high, x - high


def dot(a, b, dims=NN, precision=None):
    return lax.dot_general(a, b, dims, precision=precision, preferred_element_type=f32)


def counter(count, n):
    return jnp.concatenate([iota((count, L), 0).astype(f32).astype(bf16)] * (n // L), axis=1)


def spread(x):
    return jnp.broadcast_to(x, (16, x.shape[1])).astype(bf16)


def halves(x):
    rows = jnp.broadcast_to(x, (16, x.shape[1]))
    high = rows.astype(bf16)
    return high, (rows - high.astype(f32)).astype(bf16)


def tiled(rows, count):
    return jnp.concatenate([rows] * (count // 16), axis=0)


def hits(x, count):
    return counter(count, x.shape[1]) == tiled(spread(x), count)


def onehot(mask):
    return jnp.where(mask, jnp.ones(mask.shape, bf16), jnp.zeros(mask.shape, bf16))


def masked(mask, rows):
    return jnp.where(mask, tiled(rows, mask.shape[0]), jnp.zeros(mask.shape, bf16))


def transposed(x):
    m, n = x.shape
    if n < L:
        x = jnp.concatenate([x, jnp.zeros((m, L - n), f32)], axis=1)
    if m < L:
        x = jnp.concatenate([x, jnp.zeros((L - m, L), f32)], axis=0)
    return x.T


def edge_of(patch, point, width):
    last = point >= width - 3
    return (
        jnp.where(last, patch + 1, jnp.where(point < 3, patch - 1, -1)),
        jnp.where(last, point - (width - 8), point),
    )


def route(width, blocks, capacity):
    c = FACE_CHUNK
    steps = width // c
    per = capacity // L
    highs = blocks * per
    sub = 256

    def kernel(
        live_ref,
        patch_ref,
        point_ref,
        impinged_ref,
        load_ref,
        side_ref,
        before_ref,
        after_ref,
        weight_ref,
        op_ref,
        out_ref,
        slot_ref,
        carry,
        acc,
        spots,
        eacc,
        weight,
        first_face,
        first_side,
        leads,
    ):
        i = pl.program_id(0)
        gas = lax.axis_index("grp") == 0
        patch, point, side = patch_ref[...], point_ref[...], side_ref[...]

        @pl.when(i == 0)
        def _():
            carry[...] = jnp.zeros_like(carry)
            acc[...] = jnp.zeros_like(acc)
            eacc[...] = jnp.zeros_like(eacc)
            nl = side.shape[0]
            weight[...] = transposed(weight_ref[...])[:nl]
            first_face[0:1, :] = patch[:, :L]
            first_face[1:2, :] = point[:, :L]
            first_side[...] = side[:, :L]
            lead = jnp.where(iota((8, nl), 0) == 0, 1.0, 0.0) * jnp.where(iota((8, nl), 1) == 0, 1.0, 0.0)
            leads[0:1, :] = lead[0:1]
            for n in range(1, ITERS):
                lead = dot(lead, op_ref[...], precision=HIGHEST)
                leads[n : n + 1, :] = lead[0:1]
            leads[ITERS:, :] = lead[ITERS:]

        named = iota((blocks, c), 0) == patch
        hot = onehot(hits(patch.astype(f32), blocks))
        upto = jnp.where(iota((sub, sub), 0) <= iota((sub, sub), 1), 1.0, 0.0).astype(bf16)
        cuts = [slice(j * sub, (j + 1) * sub) for j in range(c // sub)]
        counts = dot(jnp.concatenate([hot[:, cut] for cut in cuts], axis=0), upto)
        before = carry[...]
        ranks = []
        for j, cut in enumerate(cuts):
            count = counts[j * blocks : (j + 1) * blocks]
            total = count + jnp.concatenate([before] * (sub // L), axis=1)
            ranks.append(jnp.sum(jnp.where(named[:, cut], total, 0.0), axis=0, keepdims=True))
            before = before + jnp.broadcast_to(count[:, sub - 1 :], (blocks, L))
        carry[...] = before
        rank = jnp.concatenate(ranks, axis=1).astype(i32) - 1
        slot = patch * capacity + rank
        slot_ref[...] = slot

        lane = iota((1, c), 1)
        live = (lane + i * c) < live_ref[0]
        row = side[0:1]
        ahead = jnp.where(lane == c - 1, jnp.where(i == steps - 1, 0.0, after_ref[0:1, 0:1]), pltpu.roll(row, c - 1, 1))
        behind = jnp.where(lane == 0, jnp.where(i == 0, 0.0, before_ref[0:1, L - 1 : L]), pltpu.roll(row, 1, 1))
        flux = jnp.sum(weight[:, 0:1] * side, axis=0, keepdims=True) + 0.25 * (behind + ahead - 2.0 * row)
        crystal = impinged_ref[...].astype(f32) * load_ref[...]
        value = jnp.where(live, jnp.where(gas, flux, crystal), 0.0)
        v_high, v_low = split(value)
        t_high, t_low = ((point >> 7).astype(f32), (point & (L - 1)).astype(f32))
        high = onehot(hits((slot >> 7).astype(f32), highs))
        low = hits((slot & (L - 1)).astype(f32), L)
        laid = jnp.concatenate([masked(low, x) for x in (*halves(value), spread(t_high), spread(t_low))], axis=0)
        placed = dot(laid, high, NT)
        for q in range(4):
            acc[pl.ds(q * L, L), :] += placed[q * L : (q + 1) * L]

        edge_patch, edge_point = edge_of(patch, point, width)
        edge_hot = onehot(hits(edge_patch.astype(f32), blocks))
        edge_low = iota((8, c), 0) == edge_point
        edges = jnp.concatenate([jnp.where(edge_low, x, 0.0) for x in (v_high, v_low)], axis=0).astype(bf16)
        eacc[...] += dot(edges, edge_hot, NT)

        @pl.when(i == steps - 1)
        def _():
            spots[pl.ds(0, highs), :] = (acc[:L] + acc[L : 2 * L]).T
            spots[pl.ds(highs, highs), :] = (acc[2 * L : 3 * L] * float(L) + acc[3 * L :]).T
            for r in range(per):
                for q in range(2):
                    out_ref[pl.ds(q * per + r, blocks, stride=ROWS), :] = spots[pl.ds(q * highs + r, blocks, stride=per), :]
            spot, to = iota((blocks, L), 1), iota((blocks, L), 0)
            info = transposed(eacc[0:8] + eacc[8:16])[:blocks]
            info = jnp.where((spot == 8) & gas, first_side[0:1, 0:1], info)
            info = jnp.where((spot == 9) & gas, row[:, c - 1 :], info)
            ends = (
                (10, first_face[0:1, 0:1], first_face[1:2, 0:1], live_ref[0] > 0),
                (11, patch[:, c - 1 :], point[:, c - 1 :], live_ref[0] >= width),
            )
            for at, name, target, alive in ends:
                info = jnp.where(spot == at, jnp.where((to == name) & alive, target.astype(f32), -1.0), info)
                name, target = edge_of(name, target, width)
                info = jnp.where(spot == at + 2, jnp.where((to == name) & alive, target.astype(f32), -1.0), info)
            block = lax.axis_index("blk")
            for near, columns, base in ((block - 1, first_side[...], 0), (block + 1, side[:, c - L :], L - HALO)):
                led = dot(leads[...], columns, precision=HIGHEST)
                for n in range(ITERS):
                    at = 16 + HALO * n
                    here = (spot >= at) & (spot < at + HALO) & (to == near)
                    info = jnp.where(here, pltpu.roll(led[n : n + 1], (at - base) % L, 1), info)
            out_ref[pl.ds(2 * per, blocks, stride=ROWS), :] = info

    def call(live_count, patch, point, impinged, load, side, weights, op):
        nl = side.shape[0]
        row = pl.BlockSpec((1, c), lambda i: (0, i))
        return pl.pallas_call(
            kernel,
            grid=(steps,),
            in_specs=[
                pl.BlockSpec(memory_space=pltpu.SMEM),
                row,
                row,
                row,
                row,
                pl.BlockSpec((nl, c), lambda i: (0, i)),
                pl.BlockSpec((8, L), lambda i: (0, jnp.maximum(i * (c // L) - 1, 0))),
                pl.BlockSpec((8, L), lambda i: (0, jnp.minimum((i + 1) * (c // L), width // L - 1))),
                pl.BlockSpec(weights.shape, lambda i: (0, 0)),
                pl.BlockSpec(op.shape, lambda i: (0, 0)),
            ],
            out_specs=[pl.BlockSpec((blocks * ROWS, L), lambda i: (0, 0)), row],
            out_shape=[
                jax.ShapeDtypeStruct((blocks * ROWS, L), f32),
                jax.ShapeDtypeStruct((1, width), i32),
            ],
            scratch_shapes=[
                pltpu.VMEM((blocks, L), f32),
                pltpu.VMEM((4 * L, highs), f32),
                pltpu.VMEM((2 * highs, L), f32),
                pltpu.VMEM((16, blocks), f32),
                pltpu.VMEM((nl, L), f32),
                pltpu.VMEM((8, L), i32),
                pltpu.VMEM((nl, L), f32),
                pltpu.VMEM((8, nl), f32),
            ],
            compiler_params=LARGE,
            name="route",
        )(live_count, patch, point, impinged, load, side, side, side, weights, op)

    return call


def matrices(nl, width):
    c = FACE_CHUNK
    steps = width // c
    out_rows = nl + 8
    tail = (ITERS + 1) * width // L

    def kernel(op_ref, weight_ref, side_ref, y_ref, rows_ref, coef_ref, lhs):
        i = pl.program_id(0)

        @pl.when(i == 0)
        def _():
            gas = lax.axis_index("grp") == 0
            coupling = transposed(weight_ref[...])[:nl, 1:2]
            one = op_ref[...]
            two = dot(one, one, precision=HIGHEST)
            three = dot(two, one, precision=HIGHEST)
            four = dot(two, two, precision=HIGHEST)
            main = jnp.where(gas, one, four)
            unit = jnp.where(iota((1, nl), 1) == 0, 1.0, 0.0)
            full = jnp.concatenate([main, unit, one[0:1], two[0:1], three[0:1], four[0:1], jnp.zeros((3, nl), f32)], axis=0)
            high, low = split(full)
            lhs[...] = jnp.concatenate([high, low, high, low], axis=1).astype(bf16)
            rows_ref[pl.ds(tail, 8), :] = jnp.concatenate([full[nl:], jnp.zeros((8, L - nl), f32)], axis=1)
            lead = [jnp.broadcast_to(m[0:1, 0:1], (1, L)) for m in (one, two, three, four)]
            rows_ref[pl.ds(tail + 8, 8), :] = jnp.concatenate(lead + [jnp.zeros((4, L), f32)], axis=0)
            lane = iota((nl, L), 1)
            coef = jnp.where(lane == 0, jnp.where(gas, coupling, four[:, 0:1]), 0.0)
            for k, m in ((1, three), (2, two), (3, one)):
                coef = jnp.where(lane == k, jnp.where(gas, 0.0, m[:, 0:1]), coef)
            coef_ref[...] = coef

        high, low = split(side_ref[...])
        high, low = high.astype(bf16), low.astype(bf16)
        out = dot(lhs[...], jnp.concatenate([high, high, low, low], axis=0))
        y_ref[...] = out[:nl]
        for n in range(ITERS + 1):
            part = [out[nl + n : nl + n + 1, k * L : (k + 1) * L] for k in range(c // L)]
            start = pl.multiple_of(n * (width // L) + i * (c // L), 8)
            rows_ref[pl.ds(start, c // L), :] = jnp.concatenate(part, axis=0)

    def call(op, weights, side):
        return pl.pallas_call(
            kernel,
            grid=(steps,),
            in_specs=[
                pl.BlockSpec((nl, nl), lambda i: (0, 0)),
                pl.BlockSpec(weights.shape, lambda i: (0, 0)),
                pl.BlockSpec((nl, c), lambda i: (0, i)),
            ],
            out_specs=[
                pl.BlockSpec((nl, c), lambda i: (0, i)),
                pl.BlockSpec((tail + 16, L), lambda i: (0, 0)),
                pl.BlockSpec((nl, L), lambda i: (0, 0)),
            ],
            out_shape=[
                jax.ShapeDtypeStruct((nl, width), f32),
                jax.ShapeDtypeStruct((tail + 16, L), f32),
                jax.ShapeDtypeStruct((nl, L), f32),
            ],
            scratch_shapes=[pltpu.VMEM((out_rows, 4 * nl), bf16)],
            compiler_params=MIDDLE,
            name="matrices",
        )(op, weights, side)

    return call


def gather_sum(width, blocks, capacity):
    per = capacity // L
    tall = width // L

    def kernel(x_ref, out_ref, acc):
        def step(s, nothing):
            start = pl.multiple_of(s * SLOT_STEP * ROWS, 8)
            x = x_ref[pl.ds(start, SLOT_STEP * ROWS), :]
            t = x.astype(i32)
            t_high, t_low = (t >> 7).astype(f32), (t & (L - 1)).astype(f32)
            highs, lows = [], []
            for m in range(SLOT_STEP):
                for r in range(per):
                    a, b = m * ROWS + r, m * ROWS + per + r
                    highs.append(onehot(hits(t_high[b : b + 1], tall)))
                    low = hits(t_low[b : b + 1], L)
                    lows.append(jnp.concatenate([masked(low, part) for part in halves(x[a : a + 1])], axis=0))
            placed = dot(jnp.concatenate(lows, axis=1), jnp.concatenate(highs, axis=1), NT)
            for q in range(2):
                acc[pl.ds(q * L, L), :] += placed[q * L : (q + 1) * L]
            return nothing

        info = x_ref[pl.ds(2 * per, blocks, stride=ROWS), :]
        across = transposed(info)
        lane = iota((1, L), 1)
        left = lane < blocks

        def ends(a, b):
            return jnp.where(left, a, pltpu.roll(b, blocks, 1))

        value = 0.25 * ends(pltpu.roll(across[9:10], 1, 1), pltpu.roll(across[8:9], L - 1, 1))
        target = ends(across[10:11], across[11:12]).astype(i32)
        halo = ends(across[12:13], across[13:14]).astype(i32)
        v_high, v_low = split(value)
        low = hits((target & (L - 1)).astype(f32), L)
        high = onehot(hits((target >> 7).astype(f32), tall))
        acc[...] = dot(jnp.concatenate([masked(low, x) for x in halves(value)], axis=0), high, NT)
        at = onehot(hits(halo.astype(f32), L))
        pieces = jnp.concatenate([v_high, v_low, jnp.zeros((6, L), f32)], axis=0).astype(bf16)
        edge = jnp.sum(dot(pieces, at, NT), axis=0, keepdims=True)
        edge = edge + jnp.where(lane < 8, jnp.sum(info, axis=0, keepdims=True), 0.0)

        lax.fori_loop(0, blocks // SLOT_STEP, step, 0)
        out_ref[pl.ds(0, tall), :] = (acc[:L] + acc[L:]).T
        block, source = lax.axis_index("blk"), iota((blocks, L), 0)
        rows = [edge]
        for near in (block - 1, block + 1):
            rows.append(jnp.sum(jnp.where(source == near, info, 0.0), axis=0, keepdims=True))
        out_ref[pl.ds(tall, 8), :] = jnp.concatenate(rows + [jnp.zeros((5, L), f32)], axis=0)

    def call(x):
        return pl.pallas_call(
            kernel,
            out_shape=jax.ShapeDtypeStruct((tall + 8, L), f32),
            scratch_shapes=[pltpu.VMEM((2 * L, tall), f32)],
            compiler_params=PARAMS,
            name="gather_sum",
        )(x)

    return call


def surface_lookup(width, blocks, capacity):
    per = capacity // L
    tall = width // L
    ext = tall + 16

    def kernel(mine_ref, other_ref, rows_mine, rows_other, film_ref, x_ref, out_ref, source_ref, surface_ref):
        gas = lax.axis_index("grp") == 0
        block = lax.axis_index("blk")
        lane, line = iota((ext, L), 1), iota((ext, L), 0)
        inside = (line >= 8) & (line < tall + 8)
        left = (line == 7) & (lane >= L - HALO)
        right = (line == tall + 8) & (lane < HALO)
        valid = inside | (left & (block > 0)) | (right & (block < blocks - 1))

        def extend(body, edge_left, edge_right):
            zeros = jnp.zeros((7, L), f32)
            full = jnp.concatenate([zeros, edge_left, body, edge_right, zeros], axis=0)
            return jnp.where(valid, full, 0.0)

        def lateral(x):
            ahead = pltpu.roll(x, L - 1, 1)
            ahead = jnp.where(lane == L - 1, pltpu.roll(ahead, ext - 1, 0), ahead)
            behind = pltpu.roll(x, 1, 1)
            behind = jnp.where(lane == 0, pltpu.roll(behind, 1, 0), behind)
            return behind + ahead - 2.0 * x

        mine, other = mine_ref[...], other_ref[...]
        heat, mass = jnp.where(gas, mine, other), jnp.where(gas, other, mine)
        q = heat - 0.5 * mass
        q_edge = q[tall : tall + 1]
        q = extend(q[:tall], pltpu.roll(q_edge, L - 8, 1), q_edge)
        tail = (ITERS + 1) * tall

        def rows(start, size):
            cut = pl.ds(start, size)
            return jnp.where(gas, rows_other[cut, :], rows_mine[cut, :])

        lead = rows(tail + 8, 8)
        near = jnp.where(gas, other[tall:], mine[tall:])

        def base(n):
            at = 16 + HALO * n
            edges = [pltpu.roll(near[k : k + 1], (to - at) % L, 1) for k, to in ((1, L - HALO), (2, 0))]
            return extend(rows(n * tall, tall), *edges)

        sources = []
        row = base(0)
        for n in range(1, ITERS + 1):
            sources.append(0.2 * (q + 0.5 * lateral(row)))
            row = base(n)
            for j, source in enumerate(sources):
                row = row + lead[n - 1 - j : n - j] * source
            row = jnp.where(valid, row, 0.0)
        for n in range(ITERS):
            source_ref[pl.ds(n * tall, tall), :] = sources[n][8 : tall + 8]
        wall_row = row[8 : tall + 8]
        film_new = jnp.maximum(film_ref[...] + 0.5 * (wall_row - 0.3) - 0.1 * mass[:tall], 0.0)
        surface_ref[pl.ds(0, tall), :] = wall_row
        surface_ref[pl.ds(tall, tall), :] = film_new

        high, low = split(jnp.where(gas, wall_row, film_new).T)
        table = jnp.concatenate([high, low], axis=1).astype(bf16)

        def step(s, carry):
            start = pl.multiple_of(s * SLOT_STEP * ROWS, 8)
            t = x_ref[pl.ds(start, SLOT_STEP * ROWS), :].astype(i32)
            t_high, t_low = (t >> 7).astype(f32), t & (L - 1)
            rows = [m * ROWS + per + r for m in range(SLOT_STEP) for r in range(per)]
            picked = []
            for g in range(0, len(rows), PIECE // L):
                group = rows[g : g + PIECE // L]
                highs = jnp.concatenate([onehot(hits(t_high[b : b + 1], tall)) for b in group], axis=1)
                found = dot(table, jnp.concatenate([highs, highs], axis=0))
                for k, b in enumerate(group):
                    low = iota((L, L), 0) == t_low[b : b + 1]
                    picked.append(jnp.sum(jnp.where(low, found[:, k * L : (k + 1) * L], 0.0), axis=0, keepdims=True))
            size = SLOT_STEP * per
            out_ref[pl.ds(pl.multiple_of(s * size, 8), size), :] = jnp.concatenate(picked, axis=0)
            return carry

        lax.fori_loop(0, blocks // SLOT_STEP, step, 0)

    def call(*args):
        vmem = pl.BlockSpec(memory_space=pltpu.VMEM)
        return pl.pallas_call(
            kernel,
            in_specs=[vmem] * 6,
            out_shape=[
                jax.ShapeDtypeStruct((blocks * per, L), f32),
                jax.ShapeDtypeStruct((ITERS * tall, L), f32),
                jax.ShapeDtypeStruct((2 * tall, L), f32),
            ],
            compiler_params=PARAMS,
            name="surface_lookup",
        )(*args)

    return call


def add_sources(nl, width):
    c = FACE_CHUNK
    tall = width // L
    part = c // L

    def kernel(y_ref, coef_ref, source_ref, out_ref):
        gas = lax.axis_index("grp") == 0

        @pl.when(gas)
        def _():
            out_ref[...] = y_ref[...]

        @pl.when(jnp.logical_not(gas))
        def _():
            coef = coef_ref[...]
            spread = [jnp.broadcast_to(coef[:, n : n + 1], (nl, L)) for n in range(ITERS)]
            for k in range(part):
                cut = slice(k * L, (k + 1) * L)
                total = y_ref[:, cut]
                for n in range(ITERS):
                    total = total + spread[n] * source_ref[n, k : k + 1]
                out_ref[:, cut] = total

    def call(y, coef, source):
        wide = pl.BlockSpec((nl, c), lambda i: (0, i))
        return pl.pallas_call(
            kernel,
            grid=(width // c,),
            in_specs=[
                wide,
                pl.BlockSpec((nl, L), lambda i: (0, 0)),
                pl.BlockSpec((ITERS, part, L), lambda i: (0, i, 0)),
            ],
            out_specs=wide,
            out_shape=jax.ShapeDtypeStruct((nl, width), f32),
            compiler_params=MIDDLE,
            name="add_sources",
        )(y, coef, source.reshape(ITERS, tall, L))

    return call


def face_finish(nl, width, blocks, capacity):
    c = FACE_CHUNK
    steps = width // c
    tall = width // L
    highs = blocks * capacity // L

    def kernel(live_ref, reply_ref, slot_ref, y_hbm, coef_ref, surface_ref, out_hbm, found_ref, rows_ref, buffer, arrive, leave):
        gas = lax.axis_index("grp") == 0

        def incoming(i):
            return pltpu.make_async_copy(y_hbm.at[:, pl.ds(i * c, c)], buffer.at[i], arrive.at[i])

        def outgoing(i):
            return pltpu.make_async_copy(buffer.at[i], out_hbm.at[:, pl.ds(i * c, c)], leave.at[i])

        for i in range(steps):
            incoming(i).start()
        high, low = split(reply_ref[...].T)
        table = jnp.concatenate([high, low], axis=0).astype(bf16)
        coupling = jnp.broadcast_to(jnp.where(gas, coef_ref[:, 0:1], 0.0), (nl, L))
        for i in range(steps):
            incoming(i).wait()
            for j in range(c // PIECE):
                start = i * c + j * PIECE
                piece = slice(start, start + PIECE)
                slot = slot_ref[:, piece]
                found = dot(table, onehot(hits((slot >> 7).astype(f32), highs)))
                low = iota((L, PIECE), 0) == (slot & (L - 1))
                live = (iota((1, PIECE), 1) + start) < live_ref[0]
                picked = jnp.sum(jnp.where(low, found[:L] + found[L:], 0.0), axis=0, keepdims=True)
                picked = jnp.where(live, picked, 0.0)
                found_ref[:, piece] = picked
                for k in range(PIECE // L):
                    m = start // L + k
                    cut = slice(m * L, (m + 1) * L)
                    here = slice(j * PIECE + k * L, j * PIECE + (k + 1) * L)
                    one = picked[:, k * L : (k + 1) * L]
                    buffer[i, :, here] = buffer[i, :, here] + coupling * one
                    rows_ref[0:1, cut] = jnp.where(gas, one, surface_ref[m : m + 1])
                    rows_ref[1:2, cut] = surface_ref[tall + m : tall + m + 1]
            outgoing(i).start()
        for i in range(steps):
            outgoing(i).wait()

    def call(*args):
        vmem, anywhere = pl.BlockSpec(memory_space=pltpu.VMEM), pl.BlockSpec(memory_space=pl.ANY)
        return pl.pallas_call(
            kernel,
            in_specs=[pl.BlockSpec(memory_space=pltpu.SMEM), vmem, vmem, anywhere, vmem, vmem],
            out_specs=[anywhere, vmem, vmem],
            out_shape=[
                jax.ShapeDtypeStruct((nl, width), f32),
                jax.ShapeDtypeStruct((1, width), f32),
                jax.ShapeDtypeStruct((2, width), f32),
            ],
            scratch_shapes=[
                pltpu.VMEM((steps, nl, c), f32),
                pltpu.SemaphoreType.DMA((steps,)),
                pltpu.SemaphoreType.DMA((steps,)),
            ],
            compiler_params=MIDDLE,
            name="face_finish",
        )(*args)

    return call


def local(columns, operators, normal_weights, face_patch, face_point, live_count, impinged, crystal_load, film):
    nl, width = columns.shape[1:]
    blocks = lax.axis_size("blk")
    capacity = 2 * width // blocks
    per = capacity // L
    gas = lax.axis_index("grp") == 0
    side, matrix = columns[0], operators[0]
    swap = [(i, blocks + i) for i in range(blocks)] + [(blocks + i, i) for i in range(blocks)]

    def across(x):
        return lax.ppermute(x, ("grp", "blk"), swap)

    def exchange(x):
        return lax.all_to_all(x.reshape(-1), "blk", split_axis=0, concat_axis=0, tiled=True).reshape(x.shape)

    faces = [x.reshape(1, width) for x in (face_patch, face_point, impinged, crystal_load)]
    message, slot = route(width, blocks, capacity)(live_count, *faces, side, normal_weights, matrix)
    arrived = exchange(message)
    y, rows, coef = matrices(nl, width)(matrix, normal_weights, side)
    rows_other = across(rows)

    mine = gather_sum(width, blocks, capacity)(arrived)
    film = film.reshape(width // L, L)
    replies, source, surface = surface_lookup(width, blocks, capacity)(mine, across(mine), rows, rows_other, film, arrived)
    returned = exchange(replies)
    y = add_sources(nl, width)(y, coef, source)
    new_columns, found, surface = face_finish(nl, width, blocks, capacity)(live_count, returned, slot, y, coef, surface)
    bottom = lax.broadcasted_iota(i32, surface.shape, 0) == 1
    surface = jnp.where(gas & bottom, across(found), surface)
    return new_columns[None], surface[None]


def solution(mesh):
    return jax.shard_map(
        local,
        mesh=mesh,
        in_specs=(
            P("grp", None, "blk"),
            P("grp", None, None),
            P(),
            P("blk", None),
            P("blk"),
            P("blk"),
            P("blk"),
            P("blk"),
            P("blk"),
        ),
        out_specs=(P("grp", None, "blk"), P("grp", None, "blk")),
        check_vma=False,
    )
```

```python
import jax
import jax.numpy as jnp
from jax import lax
from jax.experimental import pallas as pl
from jax.experimental.pallas import tpu as pltpu
from jax.sharding import PartitionSpec as P

ITERS = 4
L = 128
HALO = ITERS
PARAMS = pltpu.CompilerParams(vmem_limit_bytes=24 << 20)
MIDDLE = pltpu.CompilerParams(vmem_limit_bytes=52 << 20)
LARGE = pltpu.CompilerParams(vmem_limit_bytes=60 << 20)
ROWS = 9
FACE_CHUNK = 2048
PIECE = 256
SLOT_STEP = 8

f32 = jnp.float32
bf16 = jnp.bfloat16
i32 = jnp.int32
HIGHEST = lax.Precision.HIGHEST
NT = (((1,), (1,)), ((), ()))
NN = (((1,), (0,)), ((), ()))


def iota(shape, dim):
    return lax.broadcasted_iota(i32, shape, dim)


def split(x):
    high = x.astype(bf16).astype(f32)
    return high, x - high


def dot(a, b, dims=NN, precision=None):
    return lax.dot_general(a, b, dims, precision=precision, preferred_element_type=f32)


def counter(count, n):
    return jnp.concatenate([iota((count, L), 0).astype(f32).astype(bf16)] * (n // L), axis=1)


def spread(x):
    return jnp.broadcast_to(x, (16, x.shape[1])).astype(bf16)


def halves(x):
    rows = jnp.broadcast_to(x, (16, x.shape[1]))
    high = rows.astype(bf16)
    return high, (rows - high.astype(f32)).astype(bf16)


def tiled(rows, count):
    return jnp.concatenate([rows] * (count // 16), axis=0)


def hits(x, count):
    return counter(count, x.shape[1]) == tiled(spread(x), count)


def onehot(mask):
    return jnp.where(mask, jnp.ones(mask.shape, bf16), jnp.zeros(mask.shape, bf16))


def masked(mask, rows):
    return jnp.where(mask, tiled(rows, mask.shape[0]), jnp.zeros(mask.shape, bf16))


def transposed(x):
    m, n = x.shape
    if n < L:
        x = jnp.concatenate([x, jnp.zeros((m, L - n), f32)], axis=1)
    if m < L:
        x = jnp.concatenate([x, jnp.zeros((L - m, L), f32)], axis=0)
    return x.T


def edge_of(patch, point, width):
    last = point >= width - 3
    return (
        jnp.where(last, patch + 1, jnp.where(point < 3, patch - 1, -1)),
        jnp.where(last, point - (width - 8), point),
    )


def route(width, blocks, capacity):
    c = FACE_CHUNK
    steps = width // c
    per = capacity // L
    highs = blocks * per
    sub = 256

    def kernel(
        live_ref,
        patch_ref,
        point_ref,
        impinged_ref,
        load_ref,
        side_hbm,
        weight_ref,
        op_ref,
        out_ref,
        slot_ref,
        acc,
        spots,
        buffer,
        arrive,
    ):
        gas = lax.axis_index("grp") == 0
        nl = op_ref.shape[0]

        def incoming(i):
            return pltpu.make_async_copy(side_hbm.at[:, pl.ds(i * c, c)], buffer.at[i], arrive.at[i])

        for i in range(steps):
            incoming(i).start()

        wide = (sub, sub + L)
        upto = jnp.where((iota(wide, 0) <= iota(wide, 1)) | (iota(wide, 1) >= sub), 1.0, 0.0).astype(bf16)
        before = jnp.zeros((blocks, L), f32)
        for i in range(steps):
            patch = patch_ref[:, i * c : (i + 1) * c]
            named = iota((blocks, c), 0) == patch
            hot = onehot(hits(patch.astype(f32), blocks))
            cuts = [slice(j * sub, (j + 1) * sub) for j in range(c // sub)]
            counts = dot(jnp.concatenate([hot[:, cut] for cut in cuts], axis=0), upto)
            ranks = []
            for j, cut in enumerate(cuts):
                count = counts[j * blocks : (j + 1) * blocks]
                total = count[:, :sub] + jnp.concatenate([before] * (sub // L), axis=1)
                ranks.append(jnp.sum(jnp.where(named[:, cut], total, 0.0), axis=0, keepdims=True))
                before = before + count[:, sub:]
            slot_ref[:, i * c : (i + 1) * c] = patch * capacity + jnp.concatenate(ranks, axis=1).astype(i32) - 1

        weight = transposed(weight_ref[...])[:nl, 0:1]
        lead = op_ref[0:8, :]
        leads = [jnp.where(iota((1, nl), 1) == 0, 1.0, 0.0), lead[0:1]]
        for _ in range(2, ITERS):
            lead = dot(lead, op_ref[...], precision=HIGHEST)
            leads.append(lead[0:1])
        leads = jnp.concatenate(leads + [jnp.zeros((8 - ITERS, nl), f32)], axis=0)
        for i in range(steps):
            incoming(i).wait()

        eacc = jnp.zeros((16, blocks), f32)
        for i in range(steps):
            part = slice(i * c, (i + 1) * c)
            slot, point, side = slot_ref[:, part], point_ref[:, part], buffer[i]
            lane = iota((1, c), 1)
            live = (lane + i * c) < live_ref[0]
            row = side[0:1]
            after = buffer[i + 1, 0:1, 0:1] if i + 1 < steps else 0.0
            prior = buffer[i - 1, 0:1, c - L :][:, L - 1 :] if i else 0.0
            ahead = jnp.where(lane == c - 1, after, pltpu.roll(row, c - 1, 1))
            behind = jnp.where(lane == 0, prior, pltpu.roll(row, 1, 1))
            flux = jnp.sum(weight * side, axis=0, keepdims=True) + 0.25 * (behind + ahead - 2.0 * row)
            crystal = impinged_ref[:, part].astype(f32) * load_ref[:, part]
            value = jnp.where(live, jnp.where(gas, flux, crystal), 0.0)
            t_high, t_low = ((point >> 7).astype(f32), (point & (L - 1)).astype(f32))
            high = onehot(hits((slot >> 7).astype(f32), highs))
            low = hits((slot & (L - 1)).astype(f32), L)
            laid = jnp.concatenate([masked(low, x) for x in (*halves(value), spread(t_high), spread(t_low))], axis=0)
            placed = dot(laid, high, NT)
            for q in range(4):
                rows = placed[q * L : (q + 1) * L]
                acc[pl.ds(q * L, L), :] = rows if i == 0 else acc[pl.ds(q * L, L), :] + rows

            v_high, v_low = split(value)
            edge_patch, edge_point = edge_of(patch_ref[:, part], point, width)
            edge_hot = onehot(hits(edge_patch.astype(f32), blocks))
            edge_low = iota((8, c), 0) == edge_point
            edges = jnp.concatenate([jnp.where(edge_low, x, 0.0) for x in (v_high, v_low)], axis=0).astype(bf16)
            eacc = eacc + dot(edges, edge_hot, NT)

        spots[pl.ds(0, highs), :] = (acc[:L] + acc[L : 2 * L]).T
        spots[pl.ds(highs, highs), :] = (acc[2 * L : 3 * L] * float(L) + acc[3 * L :]).T
        for r in range(per):
            for q in range(2):
                out_ref[pl.ds(q * per + r, blocks, stride=ROWS), :] = spots[pl.ds(q * highs + r, blocks, stride=per), :]
        spot, to = iota((blocks, L), 1), iota((blocks, L), 0)
        info = transposed(eacc[0:8] + eacc[8:16])[:blocks]
        first, last = buffer[0, :, :L], buffer[steps - 1, :, c - L :]
        info = jnp.where((spot == 8) & gas, first[0:1, 0:1], info)
        info = jnp.where((spot == 9) & gas, last[0:1, L - 1 :], info)
        patches, points = (patch_ref[:, :L], patch_ref[:, width - L :]), (point_ref[:, :L], point_ref[:, width - L :])
        ends = (
            (10, patches[0][:, 0:1], points[0][:, 0:1], live_ref[0] > 0),
            (11, patches[1][:, L - 1 :], points[1][:, L - 1 :], live_ref[0] >= width),
        )
        for at, name, target, alive in ends:
            info = jnp.where(spot == at, jnp.where((to == name) & alive, target.astype(f32), -1.0), info)
            name, target = edge_of(name, target, width)
            info = jnp.where(spot == at + 2, jnp.where((to == name) & alive, target.astype(f32), -1.0), info)
        block = lax.axis_index("blk")
        for near, columns, base in ((block - 1, first, 0), (block + 1, last, L - HALO)):
            led = dot(leads, columns, precision=HIGHEST)
            for n in range(ITERS):
                at = 16 + HALO * n
                here = (spot >= at) & (spot < at + HALO) & (to == near)
                info = jnp.where(here, pltpu.roll(led[n : n + 1], (at - base) % L, 1), info)
        out_ref[pl.ds(2 * per, blocks, stride=ROWS), :] = info

    def call(*args):
        nl = args[5].shape[0]
        vmem, anywhere = pl.BlockSpec(memory_space=pltpu.VMEM), pl.BlockSpec(memory_space=pl.ANY)
        return pl.pallas_call(
            kernel,
            in_specs=[pl.BlockSpec(memory_space=pltpu.SMEM), vmem, vmem, vmem, vmem, anywhere, vmem, vmem],
            out_specs=[vmem, vmem],
            out_shape=[
                jax.ShapeDtypeStruct((blocks * ROWS, L), f32),
                jax.ShapeDtypeStruct((1, width), i32),
            ],
            scratch_shapes=[
                pltpu.VMEM((4 * L, highs), f32),
                pltpu.VMEM((2 * highs, L), f32),
                pltpu.VMEM((steps, nl, c), f32),
                pltpu.SemaphoreType.DMA((steps,)),
            ],
            compiler_params=LARGE,
            name="route",
        )(*args)

    return call


def matrices(nl, width):
    c = FACE_CHUNK
    steps = width // c
    out_rows = nl + 8
    tail = (ITERS + 1) * width // L

    def kernel(op_ref, weight_ref, side_ref, y_ref, rows_ref, coef_ref, lhs):
        i = pl.program_id(0)

        @pl.when(i == 0)
        def _():
            gas = lax.axis_index("grp") == 0
            coupling = transposed(weight_ref[...])[:nl, 1:2]
            one = op_ref[...]
            two = dot(one, one, precision=HIGHEST)
            three = dot(two, one, precision=HIGHEST)
            four = dot(two, two, precision=HIGHEST)
            main = jnp.where(gas, one, four)
            unit = jnp.where(iota((1, nl), 1) == 0, 1.0, 0.0)
            full = jnp.concatenate([main, unit, one[0:1], two[0:1], three[0:1], four[0:1], jnp.zeros((3, nl), f32)], axis=0)
            high, low = split(full)
            lhs[...] = jnp.concatenate([high, low, high, low], axis=1).astype(bf16)
            rows_ref[pl.ds(tail, 8), :] = jnp.concatenate([full[nl:], jnp.zeros((8, L - nl), f32)], axis=1)
            lead = [jnp.broadcast_to(m[0:1, 0:1], (1, L)) for m in (one, two, three, four)]
            rows_ref[pl.ds(tail + 8, 8), :] = jnp.concatenate(lead + [jnp.zeros((4, L), f32)], axis=0)
            lane = iota((nl, L), 1)
            coef = jnp.where(lane == 0, jnp.where(gas, coupling, four[:, 0:1]), 0.0)
            for k, m in ((1, three), (2, two), (3, one)):
                coef = jnp.where(lane == k, jnp.where(gas, 0.0, m[:, 0:1]), coef)
            coef_ref[...] = coef

        high, low = split(side_ref[...])
        high, low = high.astype(bf16), low.astype(bf16)
        out = dot(lhs[...], jnp.concatenate([high, high, low, low], axis=0))
        y_ref[...] = out[:nl]
        for n in range(ITERS + 1):
            part = [out[nl + n : nl + n + 1, k * L : (k + 1) * L] for k in range(c // L)]
            start = pl.multiple_of(n * (width // L) + i * (c // L), 8)
            rows_ref[pl.ds(start, c // L), :] = jnp.concatenate(part, axis=0)

    def call(op, weights, side):
        return pl.pallas_call(
            kernel,
            grid=(steps,),
            in_specs=[
                pl.BlockSpec((nl, nl), lambda i: (0, 0)),
                pl.BlockSpec(weights.shape, lambda i: (0, 0)),
                pl.BlockSpec((nl, c), lambda i: (0, i)),
            ],
            out_specs=[
                pl.BlockSpec((nl, c), lambda i: (0, i)),
                pl.BlockSpec((tail + 16, L), lambda i: (0, 0)),
                pl.BlockSpec((nl, L), lambda i: (0, 0)),
            ],
            out_shape=[
                jax.ShapeDtypeStruct((nl, width), f32),
                jax.ShapeDtypeStruct((tail + 16, L), f32),
                jax.ShapeDtypeStruct((nl, L), f32),
            ],
            scratch_shapes=[pltpu.VMEM((out_rows, 4 * nl), bf16)],
            compiler_params=MIDDLE,
            name="matrices",
        )(op, weights, side)

    return call


def gather_sum(width, blocks, capacity):
    per = capacity // L
    tall = width // L

    def kernel(x_ref, out_ref, acc):
        def step(s, nothing):
            start = pl.multiple_of(s * SLOT_STEP * ROWS, 8)
            x = x_ref[pl.ds(start, SLOT_STEP * ROWS), :]
            t = x.astype(i32)
            t_high, t_low = (t >> 7).astype(f32), (t & (L - 1)).astype(f32)
            highs, lows = [], []
            for m in range(SLOT_STEP):
                for r in range(per):
                    a, b = m * ROWS + r, m * ROWS + per + r
                    highs.append(onehot(hits(t_high[b : b + 1], tall)))
                    low = hits(t_low[b : b + 1], L)
                    lows.append(jnp.concatenate([masked(low, part) for part in halves(x[a : a + 1])], axis=0))
            placed = dot(jnp.concatenate(lows, axis=1), jnp.concatenate(highs, axis=1), NT)
            for q in range(2):
                acc[pl.ds(q * L, L), :] += placed[q * L : (q + 1) * L]
            return nothing

        info = x_ref[pl.ds(2 * per, blocks, stride=ROWS), :]
        across = transposed(info)
        lane = iota((1, L), 1)
        left = lane < blocks

        def ends(a, b):
            return jnp.where(left, a, pltpu.roll(b, blocks, 1))

        value = 0.25 * ends(pltpu.roll(across[9:10], 1, 1), pltpu.roll(across[8:9], L - 1, 1))
        target = ends(across[10:11], across[11:12]).astype(i32)
        halo = ends(across[12:13], across[13:14]).astype(i32)
        v_high, v_low = split(value)
        low = hits((target & (L - 1)).astype(f32), L)
        high = onehot(hits((target >> 7).astype(f32), tall))
        acc[...] = dot(jnp.concatenate([masked(low, x) for x in halves(value)], axis=0), high, NT)
        at = onehot(hits(halo.astype(f32), L))
        pieces = jnp.concatenate([v_high, v_low, jnp.zeros((6, L), f32)], axis=0).astype(bf16)
        edge = jnp.sum(dot(pieces, at, NT), axis=0, keepdims=True)
        edge = edge + jnp.where(lane < 8, jnp.sum(info, axis=0, keepdims=True), 0.0)

        lax.fori_loop(0, blocks // SLOT_STEP, step, 0)
        out_ref[pl.ds(0, tall), :] = (acc[:L] + acc[L:]).T
        block, source = lax.axis_index("blk"), iota((blocks, L), 0)
        rows = [edge]
        for near in (block - 1, block + 1):
            rows.append(jnp.sum(jnp.where(source == near, info, 0.0), axis=0, keepdims=True))
        out_ref[pl.ds(tall, 8), :] = jnp.concatenate(rows + [jnp.zeros((5, L), f32)], axis=0)

    def call(x):
        return pl.pallas_call(
            kernel,
            out_shape=jax.ShapeDtypeStruct((tall + 8, L), f32),
            scratch_shapes=[pltpu.VMEM((2 * L, tall), f32)],
            compiler_params=PARAMS,
            name="gather_sum",
        )(x)

    return call


def surface_lookup(width, blocks, capacity):
    per = capacity // L
    tall = width // L
    ext = tall + 16

    def kernel(mine_ref, other_ref, rows_mine, rows_other, film_ref, x_ref, out_ref, source_ref, surface_ref):
        gas = lax.axis_index("grp") == 0
        block = lax.axis_index("blk")
        lane, line = iota((ext, L), 1), iota((ext, L), 0)
        inside = (line >= 8) & (line < tall + 8)
        left = (line == 7) & (lane >= L - HALO)
        right = (line == tall + 8) & (lane < HALO)
        valid = inside | (left & (block > 0)) | (right & (block < blocks - 1))

        def extend(body, edge_left, edge_right):
            zeros = jnp.zeros((7, L), f32)
            full = jnp.concatenate([zeros, edge_left, body, edge_right, zeros], axis=0)
            return jnp.where(valid, full, 0.0)

        def lateral(x):
            ahead = pltpu.roll(x, L - 1, 1)
            ahead = jnp.where(lane == L - 1, pltpu.roll(ahead, ext - 1, 0), ahead)
            behind = pltpu.roll(x, 1, 1)
            behind = jnp.where(lane == 0, pltpu.roll(behind, 1, 0), behind)
            return behind + ahead - 2.0 * x

        mine, other = mine_ref[...], other_ref[...]
        heat, mass = jnp.where(gas, mine, other), jnp.where(gas, other, mine)
        q = heat - 0.5 * mass
        q_edge = q[tall : tall + 1]
        q = extend(q[:tall], pltpu.roll(q_edge, L - 8, 1), q_edge)
        tail = (ITERS + 1) * tall

        def rows(start, size):
            cut = pl.ds(start, size)
            return jnp.where(gas, rows_other[cut, :], rows_mine[cut, :])

        lead = rows(tail + 8, 8)
        near = jnp.where(gas, other[tall:], mine[tall:])

        def base(n):
            at = 16 + HALO * n
            edges = [pltpu.roll(near[k : k + 1], (to - at) % L, 1) for k, to in ((1, L - HALO), (2, 0))]
            return extend(rows(n * tall, tall), *edges)

        sources = []
        row = base(0)
        for n in range(1, ITERS + 1):
            sources.append(0.2 * (q + 0.5 * lateral(row)))
            row = base(n)
            for j, source in enumerate(sources):
                row = row + lead[n - 1 - j : n - j] * source
            row = jnp.where(valid, row, 0.0)
        for n in range(ITERS):
            source_ref[pl.ds(n * tall, tall), :] = sources[n][8 : tall + 8]
        wall_row = row[8 : tall + 8]
        film_new = jnp.maximum(film_ref[...] + 0.5 * (wall_row - 0.3) - 0.1 * mass[:tall], 0.0)
        surface_ref[pl.ds(0, tall), :] = wall_row
        surface_ref[pl.ds(tall, tall), :] = film_new

        high, low = split(jnp.where(gas, wall_row, film_new).T)
        table = jnp.concatenate([high, low], axis=1).astype(bf16)

        def step(s, carry):
            start = pl.multiple_of(s * SLOT_STEP * ROWS, 8)
            t = x_ref[pl.ds(start, SLOT_STEP * ROWS), :].astype(i32)
            t_high, t_low = (t >> 7).astype(f32), t & (L - 1)
            rows = [m * ROWS + per + r for m in range(SLOT_STEP) for r in range(per)]
            picked = []
            for g in range(0, len(rows), PIECE // L):
                group = rows[g : g + PIECE // L]
                highs = jnp.concatenate([onehot(hits(t_high[b : b + 1], tall)) for b in group], axis=1)
                found = dot(table, jnp.concatenate([highs, highs], axis=0))
                for k, b in enumerate(group):
                    low = iota((L, L), 0) == t_low[b : b + 1]
                    picked.append(jnp.sum(jnp.where(low, found[:, k * L : (k + 1) * L], 0.0), axis=0, keepdims=True))
            size = SLOT_STEP * per
            out_ref[pl.ds(pl.multiple_of(s * size, 8), size), :] = jnp.concatenate(picked, axis=0)
            return carry

        lax.fori_loop(0, blocks // SLOT_STEP, step, 0)

    def call(*args):
        vmem = pl.BlockSpec(memory_space=pltpu.VMEM)
        return pl.pallas_call(
            kernel,
            in_specs=[vmem] * 6,
            out_shape=[
                jax.ShapeDtypeStruct((blocks * per, L), f32),
                jax.ShapeDtypeStruct((ITERS * tall, L), f32),
                jax.ShapeDtypeStruct((2 * tall, L), f32),
            ],
            compiler_params=PARAMS,
            name="surface_lookup",
        )(*args)

    return call


def add_sources(nl, width):
    c = FACE_CHUNK
    tall = width // L
    part = c // L

    def kernel(y_ref, coef_ref, source_ref, out_ref):
        gas = lax.axis_index("grp") == 0

        @pl.when(gas)
        def _():
            out_ref[...] = y_ref[...]

        @pl.when(jnp.logical_not(gas))
        def _():
            coef = coef_ref[...]
            spread = [jnp.broadcast_to(coef[:, n : n + 1], (nl, L)) for n in range(ITERS)]
            for k in range(part):
                cut = slice(k * L, (k + 1) * L)
                total = y_ref[:, cut]
                for n in range(ITERS):
                    total = total + spread[n] * source_ref[n, k : k + 1]
                out_ref[:, cut] = total

    def call(y, coef, source):
        wide = pl.BlockSpec((nl, c), lambda i: (0, i))
        return pl.pallas_call(
            kernel,
            grid=(width // c,),
            in_specs=[
                wide,
                pl.BlockSpec((nl, L), lambda i: (0, 0)),
                pl.BlockSpec((ITERS, part, L), lambda i: (0, i, 0)),
            ],
            out_specs=wide,
            out_shape=jax.ShapeDtypeStruct((nl, width), f32),
            compiler_params=MIDDLE,
            name="add_sources",
        )(y, coef, source.reshape(ITERS, tall, L))

    return call


def face_finish(nl, width, blocks, capacity):
    c = FACE_CHUNK
    steps = width // c
    tall = width // L
    highs = blocks * capacity // L

    def kernel(live_ref, reply_ref, slot_ref, y_hbm, coef_ref, surface_ref, out_hbm, found_ref, rows_ref, buffer, arrive, leave):
        gas = lax.axis_index("grp") == 0

        def incoming(i):
            return pltpu.make_async_copy(y_hbm.at[:, pl.ds(i * c, c)], buffer.at[i], arrive.at[i])

        def outgoing(i):
            return pltpu.make_async_copy(buffer.at[i], out_hbm.at[:, pl.ds(i * c, c)], leave.at[i])

        for i in range(steps):
            incoming(i).start()
        high, low = split(reply_ref[...].T)
        table = jnp.concatenate([high, low], axis=0).astype(bf16)
        coupling = jnp.broadcast_to(jnp.where(gas, coef_ref[:, 0:1], 0.0), (nl, L))
        for i in range(steps):
            incoming(i).wait()
            for j in range(c // PIECE):
                start = i * c + j * PIECE
                piece = slice(start, start + PIECE)
                slot = slot_ref[:, piece]
                found = dot(table, onehot(hits((slot >> 7).astype(f32), highs)))
                low = iota((L, PIECE), 0) == (slot & (L - 1))
                live = (iota((1, PIECE), 1) + start) < live_ref[0]
                picked = jnp.sum(jnp.where(low, found[:L] + found[L:], 0.0), axis=0, keepdims=True)
                picked = jnp.where(live, picked, 0.0)
                found_ref[:, piece] = picked
                for k in range(PIECE // L):
                    m = start // L + k
                    cut = slice(m * L, (m + 1) * L)
                    here = slice(j * PIECE + k * L, j * PIECE + (k + 1) * L)
                    one = picked[:, k * L : (k + 1) * L]
                    buffer[i, :, here] = buffer[i, :, here] + coupling * one
                    rows_ref[0:1, cut] = jnp.where(gas, one, surface_ref[m : m + 1])
                    rows_ref[1:2, cut] = surface_ref[tall + m : tall + m + 1]
            outgoing(i).start()
        for i in range(steps):
            outgoing(i).wait()

    def call(*args):
        vmem, anywhere = pl.BlockSpec(memory_space=pltpu.VMEM), pl.BlockSpec(memory_space=pl.ANY)
        return pl.pallas_call(
            kernel,
            in_specs=[pl.BlockSpec(memory_space=pltpu.SMEM), vmem, vmem, anywhere, vmem, vmem],
            out_specs=[anywhere, vmem, vmem],
            out_shape=[
                jax.ShapeDtypeStruct((nl, width), f32),
                jax.ShapeDtypeStruct((1, width), f32),
                jax.ShapeDtypeStruct((2, width), f32),
            ],
            scratch_shapes=[
                pltpu.VMEM((steps, nl, c), f32),
                pltpu.SemaphoreType.DMA((steps,)),
                pltpu.SemaphoreType.DMA((steps,)),
            ],
            compiler_params=MIDDLE,
            name="face_finish",
        )(*args)

    return call


def local(columns, operators, normal_weights, face_patch, face_point, live_count, impinged, crystal_load, film):
    nl, width = columns.shape[1:]
    blocks = lax.axis_size("blk")
    capacity = 2 * width // blocks
    per = capacity // L
    gas = lax.axis_index("grp") == 0
    side, matrix = columns[0], operators[0]
    swap = [(i, blocks + i) for i in range(blocks)] + [(blocks + i, i) for i in range(blocks)]

    def across(x):
        return lax.ppermute(x, ("grp", "blk"), swap)

    def exchange(x):
        return lax.all_to_all(x.reshape(-1), "blk", split_axis=0, concat_axis=0, tiled=True).reshape(x.shape)

    faces = [x.reshape(1, width) for x in (face_patch, face_point, impinged, crystal_load)]
    message, slot = route(width, blocks, capacity)(live_count, *faces, side, normal_weights, matrix)
    arrived = exchange(message)
    y, rows, coef = matrices(nl, width)(matrix, normal_weights, side)
    rows_other = across(rows)

    mine = gather_sum(width, blocks, capacity)(arrived)
    film = film.reshape(width // L, L)
    replies, source, surface = surface_lookup(width, blocks, capacity)(mine, across(mine), rows, rows_other, film, arrived)
    returned = exchange(replies)
    y = add_sources(nl, width)(y, coef, source)
    new_columns, found, surface = face_finish(nl, width, blocks, capacity)(live_count, returned, slot, y, coef, surface)
    bottom = lax.broadcasted_iota(i32, surface.shape, 0) == 1
    surface = jnp.where(gas & bottom, across(found), surface)
    return new_columns[None], surface[None]


def solution(mesh):
    return jax.shard_map(
        local,
        mesh=mesh,
        in_specs=(
            P("grp", None, "blk"),
            P("grp", None, None),
            P(),
            P("blk", None),
            P("blk"),
            P("blk"),
            P("blk"),
            P("blk"),
            P("blk"),
        ),
        out_specs=(P("grp", None, "blk"), P("grp", None, "blk")),
        check_vma=False,
    )
```

```python
import jax
import jax.numpy as jnp
from jax import lax
from jax.experimental import pallas as pl
from jax.experimental.pallas import tpu as pltpu
from jax.sharding import PartitionSpec as P

ITERS = 4
L = 128
HALO = ITERS
PARAMS = pltpu.CompilerParams(vmem_limit_bytes=24 << 20)
MIDDLE = pltpu.CompilerParams(vmem_limit_bytes=52 << 20)
LARGE = pltpu.CompilerParams(vmem_limit_bytes=60 << 20)
ROWS = 9
FACE_CHUNK = 2048
PIECE = 256
SLOT_STEP = 32

f32 = jnp.float32
bf16 = jnp.bfloat16
i32 = jnp.int32
HIGHEST = lax.Precision.HIGHEST
NT = (((1,), (1,)), ((), ()))
NN = (((1,), (0,)), ((), ()))


def iota(shape, dim):
    return lax.broadcasted_iota(i32, shape, dim)


def split(x):
    high = x.astype(bf16).astype(f32)
    return high, x - high


def dot(a, b, dims=NN, precision=None):
    return lax.dot_general(a, b, dims, precision=precision, preferred_element_type=f32)


def counter(count, n):
    return jnp.concatenate([iota((count, L), 0).astype(f32).astype(bf16)] * (n // L), axis=1)


def spread(x):
    return jnp.broadcast_to(x, (16, x.shape[1])).astype(bf16)


def halves(x):
    rows = jnp.broadcast_to(x, (16, x.shape[1]))
    high = rows.astype(bf16)
    return high, (rows - high.astype(f32)).astype(bf16)


def tiled(rows, count):
    return jnp.concatenate([rows] * (count // 16), axis=0)


def hits(x, count):
    return counter(count, x.shape[1]) == tiled(spread(x), count)


def onehot(mask):
    return jnp.where(mask, jnp.ones(mask.shape, bf16), jnp.zeros(mask.shape, bf16))


def masked(mask, rows):
    return jnp.where(mask, tiled(rows, mask.shape[0]), jnp.zeros(mask.shape, bf16))


def transposed(x):
    m, n = x.shape
    if n < L:
        x = jnp.concatenate([x, jnp.zeros((m, L - n), f32)], axis=1)
    if m < L:
        x = jnp.concatenate([x, jnp.zeros((L - m, L), f32)], axis=0)
    return x.T


def edge_of(patch, point, width):
    last = point >= width - 3
    return (
        jnp.where(last, patch + 1, jnp.where(point < 3, patch - 1, -1)),
        jnp.where(last, point - (width - 8), point),
    )


def route(width, blocks, capacity):
    c = FACE_CHUNK
    steps = width // c
    per = capacity // L
    highs = blocks * per
    sub = 256

    def kernel(
        live_ref,
        patch_ref,
        point_ref,
        impinged_ref,
        load_ref,
        side_hbm,
        weight_ref,
        op_ref,
        out_ref,
        slot_ref,
        acc,
        spots,
        buffer,
        arrive,
    ):
        gas = lax.axis_index("grp") == 0
        nl = op_ref.shape[0]

        def incoming(i):
            return pltpu.make_async_copy(side_hbm.at[:, pl.ds(i * c, c)], buffer.at[i], arrive.at[i])

        for i in range(steps):
            incoming(i).start()

        wide = (sub, sub + L)
        upto = jnp.where((iota(wide, 0) <= iota(wide, 1)) | (iota(wide, 1) >= sub), 1.0, 0.0).astype(bf16)
        before = jnp.zeros((blocks, L), f32)
        for i in range(steps):
            patch = patch_ref[:, i * c : (i + 1) * c]
            named = iota((blocks, c), 0) == patch
            hot = onehot(hits(patch.astype(f32), blocks))
            cuts = [slice(j * sub, (j + 1) * sub) for j in range(c // sub)]
            counts = dot(jnp.concatenate([hot[:, cut] for cut in cuts], axis=0), upto)
            ranks = []
            for j, cut in enumerate(cuts):
                count = counts[j * blocks : (j + 1) * blocks]
                total = count[:, :sub] + jnp.concatenate([before] * (sub // L), axis=1)
                ranks.append(jnp.sum(jnp.where(named[:, cut], total, 0.0), axis=0, keepdims=True))
                before = before + count[:, sub:]
            slot_ref[:, i * c : (i + 1) * c] = patch * capacity + jnp.concatenate(ranks, axis=1).astype(i32) - 1

        weight = transposed(weight_ref[...])[:nl, 0:1]
        lead = op_ref[0:8, :]
        leads = [jnp.where(iota((1, nl), 1) == 0, 1.0, 0.0), lead[0:1]]
        for _ in range(2, ITERS):
            lead = dot(lead, op_ref[...], precision=HIGHEST)
            leads.append(lead[0:1])
        leads = jnp.concatenate(leads + [jnp.zeros((8 - ITERS, nl), f32)], axis=0)
        for i in range(steps):
            incoming(i).wait()

        eacc = jnp.zeros((16, blocks), f32)
        for i in range(steps):
            part = slice(i * c, (i + 1) * c)
            slot, point, side = slot_ref[:, part], point_ref[:, part], buffer[i]
            lane = iota((1, c), 1)
            live = (lane + i * c) < live_ref[0]
            row = side[0:1]
            after = buffer[i + 1, 0:1, 0:1] if i + 1 < steps else 0.0
            prior = buffer[i - 1, 0:1, c - L :][:, L - 1 :] if i else 0.0
            ahead = jnp.where(lane == c - 1, after, pltpu.roll(row, c - 1, 1))
            behind = jnp.where(lane == 0, prior, pltpu.roll(row, 1, 1))
            flux = jnp.sum(weight * side, axis=0, keepdims=True) + 0.25 * (behind + ahead - 2.0 * row)
            crystal = impinged_ref[:, part].astype(f32) * load_ref[:, part]
            value = jnp.where(live, jnp.where(gas, flux, crystal), 0.0)
            t_high, t_low = ((point >> 7).astype(f32), (point & (L - 1)).astype(f32))
            high = onehot(hits((slot >> 7).astype(f32), highs))
            low = hits((slot & (L - 1)).astype(f32), L)
            laid = jnp.concatenate([masked(low, x) for x in (*halves(value), spread(t_high), spread(t_low))], axis=0)
            placed = dot(laid, high, NT)
            for q in range(4):
                rows = placed[q * L : (q + 1) * L]
                acc[pl.ds(q * L, L), :] = rows if i == 0 else acc[pl.ds(q * L, L), :] + rows

            v_high, v_low = split(value)
            edge_patch, edge_point = edge_of(patch_ref[:, part], point, width)
            edge_hot = onehot(hits(edge_patch.astype(f32), blocks))
            edge_low = iota((8, c), 0) == edge_point
            edges = jnp.concatenate([jnp.where(edge_low, x, 0.0) for x in (v_high, v_low)], axis=0).astype(bf16)
            eacc = eacc + dot(edges, edge_hot, NT)

        spots[pl.ds(0, highs), :] = (acc[:L] + acc[L : 2 * L]).T
        spots[pl.ds(highs, highs), :] = (acc[2 * L : 3 * L] * float(L) + acc[3 * L :]).T
        for r in range(per):
            for q in range(2):
                out_ref[pl.ds(q * per + r, blocks, stride=ROWS), :] = spots[pl.ds(q * highs + r, blocks, stride=per), :]
        spot, to = iota((blocks, L), 1), iota((blocks, L), 0)
        info = transposed(eacc[0:8] + eacc[8:16])[:blocks]
        first, last = buffer[0, :, :L], buffer[steps - 1, :, c - L :]
        info = jnp.where((spot == 8) & gas, first[0:1, 0:1], info)
        info = jnp.where((spot == 9) & gas, last[0:1, L - 1 :], info)
        patches, points = (patch_ref[:, :L], patch_ref[:, width - L :]), (point_ref[:, :L], point_ref[:, width - L :])
        ends = (
            (10, patches[0][:, 0:1], points[0][:, 0:1], live_ref[0] > 0),
            (11, patches[1][:, L - 1 :], points[1][:, L - 1 :], live_ref[0] >= width),
        )
        for at, name, target, alive in ends:
            info = jnp.where(spot == at, jnp.where((to == name) & alive, target.astype(f32), -1.0), info)
            name, target = edge_of(name, target, width)
            info = jnp.where(spot == at + 2, jnp.where((to == name) & alive, target.astype(f32), -1.0), info)
        block = lax.axis_index("blk")
        for near, columns, base in ((block - 1, first, 0), (block + 1, last, L - HALO)):
            led = dot(leads, columns, precision=HIGHEST)
            for n in range(ITERS):
                at = 16 + HALO * n
                here = (spot >= at) & (spot < at + HALO) & (to == near)
                info = jnp.where(here, pltpu.roll(led[n : n + 1], (at - base) % L, 1), info)
        out_ref[pl.ds(2 * per, blocks, stride=ROWS), :] = info

    def call(*args):
        nl = args[5].shape[0]
        vmem, anywhere = pl.BlockSpec(memory_space=pltpu.VMEM), pl.BlockSpec(memory_space=pl.ANY)
        return pl.pallas_call(
            kernel,
            in_specs=[pl.BlockSpec(memory_space=pltpu.SMEM), vmem, vmem, vmem, vmem, anywhere, vmem, vmem],
            out_specs=[vmem, vmem],
            out_shape=[
                jax.ShapeDtypeStruct((blocks * ROWS, L), f32),
                jax.ShapeDtypeStruct((1, width), i32),
            ],
            scratch_shapes=[
                pltpu.VMEM((4 * L, highs), f32),
                pltpu.VMEM((2 * highs, L), f32),
                pltpu.VMEM((steps, nl, c), f32),
                pltpu.SemaphoreType.DMA((steps,)),
            ],
            compiler_params=LARGE,
            name="route",
        )(*args)

    return call


def matrices(nl, width):
    c = FACE_CHUNK
    steps = width // c
    out_rows = nl + 8
    tail = (ITERS + 1) * width // L

    def kernel(op_ref, weight_ref, side_ref, y_ref, rows_ref, coef_ref, lhs):
        i = pl.program_id(0)

        @pl.when(i == 0)
        def _():
            gas = lax.axis_index("grp") == 0
            coupling = transposed(weight_ref[...])[:nl, 1:2]
            one = op_ref[...]
            two = dot(one, one, precision=HIGHEST)
            three = dot(two, one, precision=HIGHEST)
            four = dot(two, two, precision=HIGHEST)
            main = jnp.where(gas, one, four)
            unit = jnp.where(iota((1, nl), 1) == 0, 1.0, 0.0)
            full = jnp.concatenate([main, unit, one[0:1], two[0:1], three[0:1], four[0:1], jnp.zeros((3, nl), f32)], axis=0)
            high, low = split(full)
            lhs[...] = jnp.concatenate([high, low, high, low], axis=1).astype(bf16)
            rows_ref[pl.ds(tail, 8), :] = jnp.concatenate([full[nl:], jnp.zeros((8, L - nl), f32)], axis=1)
            lead = [jnp.broadcast_to(m[0:1, 0:1], (1, L)) for m in (one, two, three, four)]
            rows_ref[pl.ds(tail + 8, 8), :] = jnp.concatenate(lead + [jnp.zeros((4, L), f32)], axis=0)
            lane = iota((nl, L), 1)
            coef = jnp.where(lane == 0, jnp.where(gas, coupling, four[:, 0:1]), 0.0)
            for k, m in ((1, three), (2, two), (3, one)):
                coef = jnp.where(lane == k, jnp.where(gas, 0.0, m[:, 0:1]), coef)
            coef_ref[...] = coef

        high, low = split(side_ref[...])
        high, low = high.astype(bf16), low.astype(bf16)
        out = dot(lhs[...], jnp.concatenate([high, high, low, low], axis=0))
        y_ref[...] = out[:nl]
        for n in range(ITERS + 1):
            part = [out[nl + n : nl + n + 1, k * L : (k + 1) * L] for k in range(c // L)]
            start = pl.multiple_of(n * (width // L) + i * (c // L), 8)
            rows_ref[pl.ds(start, c // L), :] = jnp.concatenate(part, axis=0)

    def call(op, weights, side):
        return pl.pallas_call(
            kernel,
            grid=(steps,),
            in_specs=[
                pl.BlockSpec((nl, nl), lambda i: (0, 0)),
                pl.BlockSpec(weights.shape, lambda i: (0, 0)),
                pl.BlockSpec((nl, c), lambda i: (0, i)),
            ],
            out_specs=[
                pl.BlockSpec((nl, c), lambda i: (0, i)),
                pl.BlockSpec((tail + 16, L), lambda i: (0, 0)),
                pl.BlockSpec((nl, L), lambda i: (0, 0)),
            ],
            out_shape=[
                jax.ShapeDtypeStruct((nl, width), f32),
                jax.ShapeDtypeStruct((tail + 16, L), f32),
                jax.ShapeDtypeStruct((nl, L), f32),
            ],
            scratch_shapes=[pltpu.VMEM((out_rows, 4 * nl), bf16)],
            compiler_params=MIDDLE,
            name="matrices",
        )(op, weights, side)

    return call


def gather_sum(width, blocks, capacity):
    per = capacity // L
    tall = width // L

    def kernel(x_ref, out_ref, acc):
        def step(s, nothing):
            start = pl.multiple_of(s * SLOT_STEP * ROWS, 8)
            x = x_ref[pl.ds(start, SLOT_STEP * ROWS), :]
            t = x.astype(i32)
            t_high, t_low = (t >> 7).astype(f32), (t & (L - 1)).astype(f32)
            highs, lows = [], []
            for m in range(SLOT_STEP):
                for r in range(per):
                    a, b = m * ROWS + r, m * ROWS + per + r
                    highs.append(onehot(hits(t_high[b : b + 1], tall)))
                    low = hits(t_low[b : b + 1], L)
                    lows.append(jnp.concatenate([masked(low, part) for part in halves(x[a : a + 1])], axis=0))
            placed = dot(jnp.concatenate(lows, axis=1), jnp.concatenate(highs, axis=1), NT)
            for q in range(2):
                acc[pl.ds(q * L, L), :] += placed[q * L : (q + 1) * L]
            return nothing

        info = x_ref[pl.ds(2 * per, blocks, stride=ROWS), :]
        across = transposed(info)
        lane = iota((1, L), 1)
        left = lane < blocks

        def ends(a, b):
            return jnp.where(left, a, pltpu.roll(b, blocks, 1))

        value = 0.25 * ends(pltpu.roll(across[9:10], 1, 1), pltpu.roll(across[8:9], L - 1, 1))
        target = ends(across[10:11], across[11:12]).astype(i32)
        halo = ends(across[12:13], across[13:14]).astype(i32)
        v_high, v_low = split(value)
        low = hits((target & (L - 1)).astype(f32), L)
        high = onehot(hits((target >> 7).astype(f32), tall))
        acc[...] = dot(jnp.concatenate([masked(low, x) for x in halves(value)], axis=0), high, NT)
        at = onehot(hits(halo.astype(f32), L))
        pieces = jnp.concatenate([v_high, v_low, jnp.zeros((6, L), f32)], axis=0).astype(bf16)
        edge = jnp.sum(dot(pieces, at, NT), axis=0, keepdims=True)
        edge = edge + jnp.where(lane < 8, jnp.sum(info, axis=0, keepdims=True), 0.0)

        lax.fori_loop(0, blocks // SLOT_STEP, step, 0)
        out_ref[pl.ds(0, tall), :] = (acc[:L] + acc[L:]).T
        block, source = lax.axis_index("blk"), iota((blocks, L), 0)
        rows = [edge]
        for near in (block - 1, block + 1):
            rows.append(jnp.sum(jnp.where(source == near, info, 0.0), axis=0, keepdims=True))
        out_ref[pl.ds(tall, 8), :] = jnp.concatenate(rows + [jnp.zeros((5, L), f32)], axis=0)

    def call(x):
        return pl.pallas_call(
            kernel,
            out_shape=jax.ShapeDtypeStruct((tall + 8, L), f32),
            scratch_shapes=[pltpu.VMEM((2 * L, tall), f32)],
            compiler_params=PARAMS,
            name="gather_sum",
        )(x)

    return call


def surface_lookup(width, blocks, capacity):
    per = capacity // L
    tall = width // L
    ext = tall + 16

    def kernel(mine_ref, other_ref, rows_mine, rows_other, film_ref, x_ref, out_ref, source_ref, surface_ref):
        gas = lax.axis_index("grp") == 0
        block = lax.axis_index("blk")
        lane, line = iota((ext, L), 1), iota((ext, L), 0)
        inside = (line >= 8) & (line < tall + 8)
        left = (line == 7) & (lane >= L - HALO)
        right = (line == tall + 8) & (lane < HALO)
        valid = inside | (left & (block > 0)) | (right & (block < blocks - 1))

        def extend(body, edge_left, edge_right):
            zeros = jnp.zeros((7, L), f32)
            full = jnp.concatenate([zeros, edge_left, body, edge_right, zeros], axis=0)
            return jnp.where(valid, full, 0.0)

        def lateral(x):
            ahead = pltpu.roll(x, L - 1, 1)
            ahead = jnp.where(lane == L - 1, pltpu.roll(ahead, ext - 1, 0), ahead)
            behind = pltpu.roll(x, 1, 1)
            behind = jnp.where(lane == 0, pltpu.roll(behind, 1, 0), behind)
            return behind + ahead - 2.0 * x

        mine, other = mine_ref[...], other_ref[...]
        heat, mass = jnp.where(gas, mine, other), jnp.where(gas, other, mine)
        q = heat - 0.5 * mass
        q_edge = q[tall : tall + 1]
        q = extend(q[:tall], pltpu.roll(q_edge, L - 8, 1), q_edge)
        tail = (ITERS + 1) * tall

        def rows(start, size):
            cut = pl.ds(start, size)
            return jnp.where(gas, rows_other[cut, :], rows_mine[cut, :])

        lead = rows(tail + 8, 8)
        near = jnp.where(gas, other[tall:], mine[tall:])

        def base(n):
            at = 16 + HALO * n
            edges = [pltpu.roll(near[k : k + 1], (to - at) % L, 1) for k, to in ((1, L - HALO), (2, 0))]
            return extend(rows(n * tall, tall), *edges)

        sources = []
        row = base(0)
        for n in range(1, ITERS + 1):
            sources.append(0.2 * (q + 0.5 * lateral(row)))
            row = base(n)
            for j, source in enumerate(sources):
                row = row + lead[n - 1 - j : n - j] * source
            row = jnp.where(valid, row, 0.0)
        for n in range(ITERS):
            source_ref[pl.ds(n * tall, tall), :] = sources[n][8 : tall + 8]
        wall_row = row[8 : tall + 8]
        film_new = jnp.maximum(film_ref[...] + 0.5 * (wall_row - 0.3) - 0.1 * mass[:tall], 0.0)
        surface_ref[pl.ds(0, tall), :] = wall_row
        surface_ref[pl.ds(tall, tall), :] = film_new

        high, low = split(jnp.where(gas, wall_row, film_new).T)
        table = jnp.concatenate([high, low], axis=1).astype(bf16)

        def step(s, carry):
            start = pl.multiple_of(s * SLOT_STEP * ROWS, 8)
            t = x_ref[pl.ds(start, SLOT_STEP * ROWS), :].astype(i32)
            t_high, t_low = (t >> 7).astype(f32), t & (L - 1)
            rows = [m * ROWS + per + r for m in range(SLOT_STEP) for r in range(per)]
            picked = []
            for g in range(0, len(rows), PIECE // L):
                group = rows[g : g + PIECE // L]
                highs = jnp.concatenate([onehot(hits(t_high[b : b + 1], tall)) for b in group], axis=1)
                found = dot(table, jnp.concatenate([highs, highs], axis=0))
                for k, b in enumerate(group):
                    low = iota((L, L), 0) == t_low[b : b + 1]
                    picked.append(jnp.sum(jnp.where(low, found[:, k * L : (k + 1) * L], 0.0), axis=0, keepdims=True))
            size = SLOT_STEP * per
            out_ref[pl.ds(pl.multiple_of(s * size, 8), size), :] = jnp.concatenate(picked, axis=0)
            return carry

        lax.fori_loop(0, blocks // SLOT_STEP, step, 0)

    def call(*args):
        vmem = pl.BlockSpec(memory_space=pltpu.VMEM)
        return pl.pallas_call(
            kernel,
            in_specs=[vmem] * 6,
            out_shape=[
                jax.ShapeDtypeStruct((blocks * per, L), f32),
                jax.ShapeDtypeStruct((ITERS * tall, L), f32),
                jax.ShapeDtypeStruct((2 * tall, L), f32),
            ],
            compiler_params=PARAMS,
            name="surface_lookup",
        )(*args)

    return call


def add_sources(nl, width):
    c = FACE_CHUNK
    tall = width // L
    part = c // L

    def kernel(y_ref, coef_ref, source_ref, out_ref):
        gas = lax.axis_index("grp") == 0

        @pl.when(gas)
        def _():
            out_ref[...] = y_ref[...]

        @pl.when(jnp.logical_not(gas))
        def _():
            coef = coef_ref[...]
            spread = [jnp.broadcast_to(coef[:, n : n + 1], (nl, L)) for n in range(ITERS)]
            for k in range(part):
                cut = slice(k * L, (k + 1) * L)
                total = y_ref[:, cut]
                for n in range(ITERS):
                    total = total + spread[n] * source_ref[n, k : k + 1]
                out_ref[:, cut] = total

    def call(y, coef, source):
        wide = pl.BlockSpec((nl, c), lambda i: (0, i))
        return pl.pallas_call(
            kernel,
            grid=(width // c,),
            in_specs=[
                wide,
                pl.BlockSpec((nl, L), lambda i: (0, 0)),
                pl.BlockSpec((ITERS, part, L), lambda i: (0, i, 0)),
            ],
            out_specs=wide,
            out_shape=jax.ShapeDtypeStruct((nl, width), f32),
            compiler_params=MIDDLE,
            name="add_sources",
        )(y, coef, source.reshape(ITERS, tall, L))

    return call


def face_finish(nl, width, blocks, capacity):
    c = FACE_CHUNK
    steps = width // c
    tall = width // L
    highs = blocks * capacity // L

    def kernel(live_ref, reply_ref, slot_ref, y_hbm, coef_ref, surface_ref, out_hbm, found_ref, rows_ref, buffer, arrive, leave):
        gas = lax.axis_index("grp") == 0

        def incoming(i):
            return pltpu.make_async_copy(y_hbm.at[:, pl.ds(i * c, c)], buffer.at[i], arrive.at[i])

        def outgoing(i):
            return pltpu.make_async_copy(buffer.at[i], out_hbm.at[:, pl.ds(i * c, c)], leave.at[i])

        for i in range(steps):
            incoming(i).start()
        high, low = split(reply_ref[...].T)
        table = jnp.concatenate([high, low], axis=0).astype(bf16)
        coupling = jnp.broadcast_to(jnp.where(gas, coef_ref[:, 0:1], 0.0), (nl, L))
        for i in range(steps):
            incoming(i).wait()
            for j in range(c // PIECE):
                start = i * c + j * PIECE
                piece = slice(start, start + PIECE)
                slot = slot_ref[:, piece]
                found = dot(table, onehot(hits((slot >> 7).astype(f32), highs)))
                low = iota((L, PIECE), 0) == (slot & (L - 1))
                live = (iota((1, PIECE), 1) + start) < live_ref[0]
                picked = jnp.sum(jnp.where(low, found[:L] + found[L:], 0.0), axis=0, keepdims=True)
                picked = jnp.where(live, picked, 0.0)
                found_ref[:, piece] = picked
                for k in range(PIECE // L):
                    m = start // L + k
                    cut = slice(m * L, (m + 1) * L)
                    here = slice(j * PIECE + k * L, j * PIECE + (k + 1) * L)
                    one = picked[:, k * L : (k + 1) * L]
                    buffer[i, :, here] = buffer[i, :, here] + coupling * one
                    rows_ref[0:1, cut] = jnp.where(gas, one, surface_ref[m : m + 1])
                    rows_ref[1:2, cut] = surface_ref[tall + m : tall + m + 1]
            outgoing(i).start()
        for i in range(steps):
            outgoing(i).wait()

    def call(*args):
        vmem, anywhere = pl.BlockSpec(memory_space=pltpu.VMEM), pl.BlockSpec(memory_space=pl.ANY)
        return pl.pallas_call(
            kernel,
            in_specs=[pl.BlockSpec(memory_space=pltpu.SMEM), vmem, vmem, anywhere, vmem, vmem],
            out_specs=[anywhere, vmem, vmem],
            out_shape=[
                jax.ShapeDtypeStruct((nl, width), f32),
                jax.ShapeDtypeStruct((1, width), f32),
                jax.ShapeDtypeStruct((2, width), f32),
            ],
            scratch_shapes=[
                pltpu.VMEM((steps, nl, c), f32),
                pltpu.SemaphoreType.DMA((steps,)),
                pltpu.SemaphoreType.DMA((steps,)),
            ],
            compiler_params=MIDDLE,
            name="face_finish",
        )(*args)

    return call


def local(columns, operators, normal_weights, face_patch, face_point, live_count, impinged, crystal_load, film):
    nl, width = columns.shape[1:]
    blocks = lax.axis_size("blk")
    capacity = 2 * width // blocks
    per = capacity // L
    gas = lax.axis_index("grp") == 0
    side, matrix = columns[0], operators[0]
    swap = [(i, blocks + i) for i in range(blocks)] + [(blocks + i, i) for i in range(blocks)]

    def across(x):
        return lax.ppermute(x, ("grp", "blk"), swap)

    def exchange(x):
        return lax.all_to_all(x.reshape(-1), "blk", split_axis=0, concat_axis=0, tiled=True).reshape(x.shape)

    faces = [x.reshape(1, width) for x in (face_patch, face_point, impinged, crystal_load)]
    message, slot = route(width, blocks, capacity)(live_count, *faces, side, normal_weights, matrix)
    arrived = exchange(message)
    y, rows, coef = matrices(nl, width)(matrix, normal_weights, side)
    rows_other = across(rows)

    mine = gather_sum(width, blocks, capacity)(arrived)
    film = film.reshape(width // L, L)
    replies, source, surface = surface_lookup(width, blocks, capacity)(mine, across(mine), rows, rows_other, film, arrived)
    returned = exchange(replies)
    y = add_sources(nl, width)(y, coef, source)
    new_columns, found, surface = face_finish(nl, width, blocks, capacity)(live_count, returned, slot, y, coef, surface)
    bottom = lax.broadcasted_iota(i32, surface.shape, 0) == 1
    surface = jnp.where(gas & bottom, across(found), surface)
    return new_columns[None], surface[None]


def solution(mesh):
    return jax.shard_map(
        local,
        mesh=mesh,
        in_specs=(
            P("grp", None, "blk"),
            P("grp", None, None),
            P(),
            P("blk", None),
            P("blk"),
            P("blk"),
            P("blk"),
            P("blk"),
            P("blk"),
        ),
        out_specs=(P("grp", None, "blk"), P("grp", None, "blk")),
        check_vma=False,
    )
```
